256 devices in a mesh: box: 64 (over x, z, core), blk: 4 (over y).
Axes of the slice: x: 4, y: 4, z: 8, core: 2. Of those that a mesh axis runs over, the one named last changes fastest.
Arguments:
- operator_map: float32 [64, 1536, 1536], P('box', 'blk'), may hold values from -0.5 to 2, as said below
- face_list: int32 [64, 256], replicated, may hold values from 0 to 1535, as said below
Outputs:
- merged: float32 [64, 1536, 3072], P('box', 'blk')
The draws below stay inside these ranges and needn't reach their ends.
Inputs may be any that keep to these rules, and one draw needn't show every extreme that they name: `operator_map`: each box's map is symmetric; its diagonal lies in 1 to 2. Points 6 i + f and 6 j + f with the same f lie on one face: their entry is zero unless |i - j| is 1 or 2, and then lies in -0.245 to -0.12. Entries between points of different faces lie in -0.5 to 0.5. `face_list`: entry i of box b's list is 6 i + f_b with f_b from 0 to 5, so each list rises; boxes 2p and 2p + 1 list opposite faces, f = 2 a + 1 and f = 2 a, with one a from 0 to 2 for each pair, entry i of one facing entry i of the other.
All inputs are finite; a program needn't handle non-finite values.
Results may differ from the reference program's by a relative error of at most 0.0003.
Values sent between devices are 32-bit elements; how exact they have to be, the bound alone decides.
A program may use at most 64 MiB of HBM per device.

```python
import jax
import jax.numpy as jnp
from jax import lax

F = 256
M = 1536
BOXES = 64


def shared_faces(key):
    pairs = BOXES // 2
    picked_axis = jax.random.randint(jax.random.fold_in(key, 21), (pairs,), 0, 3)
    picked_axis = picked_axis.at[0].set(2).at[1].set(0)
    return jnp.stack([2 * picked_axis + 1, 2 * picked_axis], axis=1).reshape(BOXES).astype(jnp.int32)


def draw_operator_map(key, part):
    cross_key = jax.random.fold_in(key, 11)
    strength_key = jax.random.fold_in(key, 12)
    diagonal_key = jax.random.fold_in(key, 13)
    points = jnp.arange(M, dtype=jnp.int32)
    face_of = points % 6
    place = points // 6
    same_face = face_of[:, None] == face_of[None, :]
    spacing = jnp.abs(place[:, None] - place[None, :])
    nearby = jnp.logical_and(same_face, jnp.logical_or(spacing == 1, spacing == 2))
    identity = points[:, None] == points[None, :]
    upper_half = points[:, None] <= points[None, :]
    faces = shared_faces(key)
    on_shared = face_of[None, :] == faces[:, None]
    shared_entry = jnp.logical_and(on_shared[:, :, None], on_shared[:, None, :])
    strength_draw = jax.random.uniform(strength_key, (BOXES, M, M), jnp.float32, 0.0, 1.0)
    cross = jnp.clip(0.15 * jax.random.normal(cross_key, (BOXES, M, M), jnp.float32), -0.5, 0.5)
    strength_other = 0.5 + 0.5 * strength_draw
    strength = jnp.where(shared_entry, 0.99 + 0.01 * strength_draw, strength_other)
    cross = jnp.where(upper_half[None, :, :], cross, jnp.swapaxes(cross, 1, 2))
    strength = jnp.where(upper_half[None, :, :], strength, jnp.swapaxes(strength, 1, 2))
    diagonal_draw = jax.random.uniform(diagonal_key, (BOXES, M), jnp.float32, 0.0, 1.0)
    diagonal = jnp.where(on_shared, 1.0 + 0.01 * diagonal_draw, 1.0 + diagonal_draw)
    coupling = -0.245 * strength
    off_part = jnp.where(nearby[None, :, :], coupling, jnp.where(same_face[None, :, :], jnp.float32(0.0), cross))
    return jnp.where(identity[None, :, :], diagonal[:, :, None], off_part).astype(jnp.float32)


def draw_face_list(key, part):
    faces = shared_faces(key)
    positions = jnp.arange(F, dtype=jnp.int32)
    return (6 * positions[None, :] + faces[:, None]).astype(jnp.int32)


def setup_inputs(seed: int = 0) -> dict:
    arg_keys = jax.random.split(jax.random.key(seed), 3)
    return {
        "operator_map": draw_operator_map(jax.random.fold_in(arg_keys[2], 71), 0),
        "face_list": draw_face_list(jax.random.fold_in(arg_keys[2], 71), 0),
    }


def merge_pair(pair_input):
    pair_maps, pair_lists = pair_input
    lower_map = pair_maps[0]
    upper_map = pair_maps[1]
    lower_list = pair_lists[0]
    upper_list = pair_lists[1]
    lower_face = jnp.take(lower_map, lower_list, axis=0)
    upper_face = jnp.take(upper_map, upper_list, axis=0)
    schur_sum = jnp.take(lower_face, lower_list, axis=1) + jnp.take(upper_face, upper_list, axis=1)
    factor = jnp.linalg.cholesky(schur_sum)
    solved = jax.scipy.linalg.cho_solve((factor, True), jnp.concatenate([lower_face, upper_face], axis=1))
    blank = jnp.zeros_like(lower_map)
    lower_coupling = jnp.take(lower_map, lower_list, axis=1)
    upper_coupling = jnp.take(upper_map, upper_list, axis=1)
    lower_out = jnp.concatenate([lower_map, blank], axis=1) - jnp.dot(lower_coupling, solved, precision=lax.Precision.HIGHEST, preferred_element_type=lower_map.dtype)
    upper_out = jnp.concatenate([blank, upper_map], axis=1) - jnp.dot(upper_coupling, solved, precision=lax.Precision.HIGHEST, preferred_element_type=upper_map.dtype)
    return jnp.stack([lower_out, upper_out])

def reference(operator_map, face_list):
    paired_maps = operator_map.reshape(BOXES // 2, 2, M, M)
    paired_lists = face_list.reshape(BOXES // 2, 2, F)
    result = lax.map(merge_pair, (paired_maps, paired_lists))
    return result.reshape(BOXES, M, 2 * M)
```

```python
import functools

import jax
import jax.numpy as jnp
from jax import lax
from jax.experimental import pallas as pl
from jax.experimental.pallas import tpu as pltpu
from jax.sharding import PartitionSpec as P

F32 = jnp.float32
BF16 = jnp.bfloat16
LANES = 128


def split_two(x):
    high = x.astype(BF16)
    low = (x - high.astype(F32)).astype(BF16)
    return high, low


def dot(a, b):
    return jnp.dot(a, b, preferred_element_type=F32)


def kernel(
    nblk,
    map_hbm,
    list_hbm,
    out,
    kv,
    faces,
    pick,
    coupling,
    turned,
    weights,
    band_send,
    band_recv,
    coef,
    last,
    lists,
    load_sem,
    band_ssem,
    band_rsem,
    ring_ssem,
    ring_rsem,
    die_ssem,
    die_rsem,
):
    tiles, rows, _ = kv.shape
    points = tiles * LANES
    face_size = pick.shape[1]
    half = face_size // 2
    per = half // nblk
    stride = points // face_size
    box = lax.axis_index("box")
    y = lax.axis_index("blk")
    core = lax.rem(box, 2)
    mate = box + 1 - 2 * core
    ys = [lax.rem(y + d, nblk) for d in range(nblk)]
    down, up, sibling = {"blk": ys[3]}, {"blk": ys[1]}, {"box": mate}

    peers = []
    for side in range(2):
        for d in range(nblk):
            if side or d:
                peers.append((side * nblk + d, {"box": mate if side else box, "blk": ys[d]}))
    barrier = pltpu.get_barrier_semaphore()
    for _, peer in peers:
        pl.semaphore_signal(barrier, inc=1, device_id=peer)
    group = pl.multiple_of((box // 8) * 8, 8)
    load_list = pltpu.make_async_copy(
        list_hbm.at[pl.ds(group, 8), pl.ds(0, 128)], lists, load_sem.at[0]
    )
    load_list.start()
    loads = []
    for t in range(tiles):
        load = pltpu.make_async_copy(
            map_hbm.at[0, :, pl.ds(t * LANES, LANES)], kv.at[t], load_sem.at[1 + t]
        )
        load.start()
        loads.append(load)

    load_list.wait()
    f = lists[lax.rem(box, 8), 0]
    column = lax.broadcasted_iota(jnp.int32, (points, face_size), 1)
    point = lax.broadcasted_iota(jnp.int32, (points, face_size), 0)
    target = 2 * stride * lax.rem(column, half) + stride * (column // half)
    pick[...] = jnp.where(point - target == f, 1.0, 0.0).astype(BF16)

    def strip(c):
        return pl.ds(pl.multiple_of(c * per, per), per)

    def cols(c):
        return pl.ds(pl.multiple_of(c * rows, rows), rows)

    for load in loads:
        load.wait()
    mine = []
    for par in range(2):
        picked = [kv[t, pl.ds(f + stride * par, per, stride=2 * stride), :] for t in range(tiles)]
        mine.append(jnp.concatenate(picked, axis=1))
        faces[0, par, strip(y), :] = mine[par]

    pl.semaphore_wait(barrier, len(peers))

    started = []

    def send(src, dst, ssem, rsem, who):
        copy = pltpu.make_async_remote_copy(
            src_ref=src, dst_ref=dst, send_sem=ssem, recv_sem=rsem, device_id=who
        )
        copy.start()
        started.append(copy)

    def block(slot, fy, ry):
        return faces.at[slot, :, strip(fy), cols(ry)]

    def half_block(slot, par, fy, ry):
        return faces.at[slot, par, strip(fy), cols(ry)]

    def ring(way, k, ref):
        send(ref, ref, ring_ssem.at[way, k], ring_rsem.at[way, k], (down, up)[way])

    def ring_wait(way, k, ref):
        pltpu.make_async_remote_copy(
            src_ref=ref,
            dst_ref=ref,
            send_sem=ring_ssem.at[way, k],
            recv_sem=ring_rsem.at[way, k],
            device_id=(down, up)[way],
        ).wait_recv()

    def across(k, ref_of):
        send(ref_of(0), ref_of(1), die_ssem.at[k], die_rsem.at[k], sibling)

    def across_wait(k, ref_of):
        pltpu.make_async_remote_copy(
            src_ref=ref_of(0),
            dst_ref=ref_of(1),
            send_sem=die_ssem.at[k],
            recv_sem=die_rsem.at[k],
            device_id=sibling,
        ).wait_recv()

    ring(0, 0, block(0, y, y))
    ring(1, 0, block(0, y, y))

    lane = lax.broadcasted_iota(jnp.int32, (per, points), 1)
    line = lax.broadcasted_iota(jnp.int32, (per, points), 0)
    place = lane - 2 * stride * (line + per * y) - f
    bands = []
    for off in range(3):
        total = jnp.zeros((1, points), F32)
        for par in range(2):
            hit = jnp.where(place == stride * (off + par), mine[par], 0.0)
            total += jnp.sum(hit, axis=0, keepdims=True)
        bands.append(total)
    spread = jnp.concatenate(bands + [jnp.zeros((5, points), F32)], axis=0)
    packed = jnp.zeros((8, face_size), F32)
    for _ in range(3):
        term = spread.astype(BF16)
        packed += dot(term, pick[...])
        spread = spread - term.astype(F32)
    band_send[...] = packed
    for k, peer in peers:
        send(band_send, band_recv.at[k], band_ssem.at[k], band_rsem.at[k], peer)

    ring(0, 1, block(0, y, ys[2]))
    ring(1, 1, block(0, y, ys[2]))
    across(0, lambda s: faces.at[s, :, strip(y), :])

    def select(i, carry):
        part = pl.ds(pl.multiple_of(i * 128, 128), 128)
        high, low = split_two(jnp.concatenate([kv[t, part, :] for t in range(tiles)], axis=1))
        coupling[part, :] = dot(high, pick[...]) + dot(low, pick[...])
        return carry

    lax.fori_loop(0, rows // 128, select, 0)
    flipped = coupling[...].T
    for par in range(2):
        turned[par] = flipped[par * half:(par + 1) * half]
    for d in range(1, nblk):
        for par in range(2):
            faces[0, par, strip(ys[d]), cols(y)] = turned[par, strip(ys[d]), :]

    ring(0, 2, block(0, ys[1], y))
    ring(1, 2, block(0, ys[3], y))
    for d in range(1, nblk):
        across(d, lambda s, d=d: block(s, ys[d], y))

    def first(s):
        return block(s, ys[1], ys[1])

    def second(s):
        return block(s, ys[3], ys[3])

    ring_wait(0, 0, first(0))
    ring(0, 3, half_block(0, 0, ys[1], ys[1]))
    across(4, first)
    ring_wait(1, 0, second(0))
    ring(1, 3, half_block(0, 1, ys[3], ys[3]))
    across(5, second)
    ring(0, 4, block(0, y, ys[1]))
    ring(1, 4, block(0, y, ys[3]))

    for k, peer in peers:
        pltpu.make_async_remote_copy(
            src_ref=band_send,
            dst_ref=band_recv.at[k],
            send_sem=band_ssem.at[k],
            recv_sem=band_rsem.at[k],
            device_id=peer,
        ).wait_recv()
    schur = band_send[...]
    for k, _ in peers:
        schur += band_recv[k]

    def wide(r, h):
        return jnp.broadcast_to(schur[r:r + 1, h * half:(h + 1) * half], (8, half))

    a, b, c = wide(0, 0), wide(1, 1), wide(0, 1)
    l00, l01, l10, l11 = wide(2, 0), wide(1, 0), jnp.zeros((8, half), F32), wide(2, 1)
    steps = half.bit_length() - 1
    for step in range(steps):
        s = 1 << step

        def before(x, s=s):
            return pltpu.roll(x, s, 1)

        def after(x, s=s):
            return pltpu.roll(x, half - s, 1)

        scale = 1.0 / (a * c - b * b)
        ia, ib, ic = c * scale, -b * scale, a * scale
        iam, ibm, icm = before(ia), before(ib), before(ic)
        iap, ibp, icp = after(ia), after(ib), after(ic)
        m00, m01, m10, m11 = before(l00), before(l01), before(l10), before(l11)
        p00, p01, p10, p11 = after(l00), after(l01), after(l10), after(l11)
        g00, g01 = -(l00 * iam + l01 * ibm), -(l00 * ibm + l01 * icm)
        g10, g11 = -(l10 * iam + l11 * ibm), -(l10 * ibm + l11 * icm)
        h00, h01 = -(p00 * iap + p10 * ibp), -(p00 * ibp + p10 * icp)
        h10, h11 = -(p01 * iap + p11 * ibp), -(p01 * ibp + p11 * icp)
        for k, value in enumerate((g00, g01, g10, g11, h00, h01, h10, h11)):
            coef[step, k] = value
        a = a + g00 * l00 + g01 * l01 + h00 * p00 + h01 * p10
        b = b + g00 * l10 + g01 * l11 + h00 * p01 + h01 * p11
        c = c + g10 * l10 + g11 * l11 + h10 * p01 + h11 * p11
        l00, l01, l10, l11 = (
            g00 * m00 + g01 * m10,
            g00 * m01 + g01 * m11,
            g10 * m00 + g11 * m10,
            g10 * m01 + g11 * m11,
        )
    scale = 1.0 / (a * c - b * b)
    for k, value in enumerate((c * scale, -b * scale, a * scale)):
        last[k] = value

    tall = 8

    def solve(i, carry):
        part = pl.ds(pl.multiple_of(i * 8 * tall, 8 * tall), 8 * tall)
        even = coupling[part, 0:half].reshape(tall, 8, half)
        odd = coupling[part, half:].reshape(tall, 8, half)
        for step in range(steps):
            s = 1 << step
            em, om = pltpu.roll(even, s, 2), pltpu.roll(odd, s, 2)
            ep, op = pltpu.roll(even, half - s, 2), pltpu.roll(odd, half - s, 2)
            g00, g01, g10, g11, h00, h01, h10, h11 = (coef[step, k] for k in range(8))
            even, odd = (
                even + g00 * em + g01 * om + h00 * ep + h01 * op,
                odd + g10 * em + g11 * om + h10 * ep + h11 * op,
            )
        wide_e = (last[0] * even + last[1] * odd).reshape(8 * tall, half)
        wide_o = (last[1] * even + last[2] * odd).reshape(8 * tall, half)
        for h, value in enumerate((wide_e, wide_o)):
            high, low = split_two(value)
            weights[0, part, h * half:(h + 1) * half] = high
            weights[1, part, h * half:(h + 1) * half] = low
        return carry

    lax.fori_loop(0, rows // (8 * tall), solve, 0)

    def merge(slot, ry):
        high, low = split_two(faces[slot, :, :, cols(ry)].reshape(face_size, rows))
        total = dot(weights[0], high) + dot(weights[1], high) + dot(weights[0], low)
        side = core if slot == 0 else 1 - core
        place = pl.ds(pl.multiple_of(points * side + ry * rows, rows), rows)
        if slot == 0:
            wide_rows = rows // LANES
            own = [kv[ry * wide_rows + t] for t in range(wide_rows)]
            out[0, :, place] = jnp.concatenate(own, axis=1) - total
        else:
            out[0, :, place] = -total

    merge(0, y)
    across_wait(0, lambda s: faces.at[s, :, strip(y), :])
    for d in range(1, nblk):
        across_wait(d, lambda s, d=d: block(s, ys[d], y))
    merge(1, y)

    down_far = lambda s: block(s, ys[1], ys[3])
    up_far = lambda s: block(s, ys[3], ys[1])
    down_cross = lambda s: block(s, ys[2], ys[1])
    up_cross = lambda s: block(s, ys[2], ys[3])
    down_half = lambda s: half_block(s, 0, ys[2], ys[2])
    up_half = lambda s: half_block(s, 1, ys[2], ys[2])
    down_last = lambda s: block(s, ys[1], ys[2])
    up_last = lambda s: block(s, ys[3], ys[2])
    order = [
        (0, 1, down_far), (1, 1, up_far), (0, 2, down_cross), (1, 2, up_cross),
        (0, 3, down_half), (1, 3, up_half), (0, 4, down_last), (1, 4, up_last),
    ]
    for n, (way, k, ref_of) in enumerate(order):
        ring_wait(way, k, ref_of(0))
        across(6 + n, ref_of)
        if n == 3:
            merge(0, ys[1])
            merge(0, ys[3])
    across_wait(4, first)
    across_wait(5, second)
    for n in range(4):
        across_wait(6 + n, order[n][2])
    merge(1, ys[1])
    merge(1, ys[3])
    merge(0, ys[2])
    for n in range(4, 8):
        across_wait(6 + n, order[n][2])
    merge(1, ys[2])

    for copy in started:
        copy.wait_send()


def solution(mesh):
    nblk = mesh.shape["blk"]

    def on_device(operator_map, face_list):
        _, rows, points = operator_map.shape
        face_size = face_list.shape[1]
        half = face_size // 2
        steps = half.bit_length() - 1
        dma = pltpu.SemaphoreType.DMA
        return pl.pallas_call(
            functools.partial(kernel, nblk),
            out_shape=OUT((1, rows, 2 * points), F32),
            in_specs=[pl.BlockSpec(memory_space=pltpu.HBM)] * 2,
            out_specs=pl.BlockSpec(memory_space=pltpu.VMEM),
            scratch_shapes=[
                pltpu.VMEM((points // LANES, rows, LANES), F32),
                pltpu.VMEM((2, 2, half, points), F32),
                pltpu.VMEM((points, face_size), BF16),
                pltpu.VMEM((rows, face_size), F32),
                pltpu.VMEM((2, half, rows), F32),
                pltpu.VMEM((2, rows, face_size), BF16),
                pltpu.VMEM((8, face_size), F32),
                pltpu.VMEM((2 * nblk, 8, face_size), F32),
                pltpu.VMEM((steps, 8, 8, half), F32),
                pltpu.VMEM((3, 8, half), F32),
                pltpu.SMEM((8, 128), jnp.int32),
                dma((1 + points // LANES,)),
                dma((2 * nblk,)),
                dma((2 * nblk,)),
                dma((2, 5)),
                dma((2, 5)),
                dma((14,)),
                dma((14,)),
            ],
            compiler_params=pltpu.CompilerParams(
                collective_id=0, has_side_effects=True, vmem_limit_bytes=36 << 20
            ),
            name="merge_pair",
        )(operator_map, face_list)

    in_specs = (P("box", "blk", None), P())
    out_specs = P("box", "blk", None)
    return jax.shard_map(on_device, mesh=mesh, in_specs=in_specs, out_specs=out_specs, check_vma=False)


OUT = pltpu.VMEM
```

```python
import functools

import jax
import jax.numpy as jnp
from jax import lax
from jax.experimental import pallas as pl
from jax.experimental.pallas import tpu as pltpu
from jax.sharding import PartitionSpec as P

F32 = jnp.float32
BF16 = jnp.bfloat16
LANES = 128
GRANT = 51500


def split_two(x):
    high = x.astype(BF16)
    low = (x - high.astype(F32)).astype(BF16)
    return high, low


def dot(a, b):
    return jnp.dot(a, b, preferred_element_type=F32)


def product(weights, right):
    high, low = split_two(right)
    return dot(weights[0], high) + dot(weights[1], high) + dot(weights[0], low)


def kernel(
    nblk,
    map_hbm,
    list_hbm,
    out,
    weights,
    faces,
    kv,
    pick,
    coupling,
    turned,
    stage,
    band_send,
    band_sum,
    band_recv,
    coef,
    last,
    lists,
    load_sem,
    band_ssem,
    band_rsem,
    ring_ssem,
    ring_rsem,
    die_ssem,
    die_rsem,
):
    tiles, rows, _ = kv.shape
    points = tiles * LANES
    face_size = pick.shape[1]
    half = face_size // 2
    per = half // nblk
    stride = points // face_size
    box = lax.axis_index("box")
    y = lax.axis_index("blk")
    core = lax.rem(box, 2)
    mate = box + 1 - 2 * core
    ys = [lax.rem(y + d, nblk) for d in range(nblk)]
    down, up, sibling = {"blk": ys[3]}, {"blk": ys[1]}, {"box": mate}

    peers = [(d, {"blk": ys[d]}) for d in range(1, nblk)] + [(0, {"box": mate})]
    barrier = pltpu.get_barrier_semaphore()
    for _, peer in peers:
        pl.semaphore_signal(barrier, inc=1, device_id=peer)
    group = pl.multiple_of((box // 8) * 8, 8)
    load_list = pltpu.make_async_copy(
        list_hbm.at[pl.ds(group, 8), pl.ds(0, 128)], lists, load_sem.at[0]
    )
    load_list.start()
    loads = []
    for t in range(tiles):
        load = pltpu.make_async_copy(
            map_hbm.at[0, :, pl.ds(t * LANES, LANES)], kv.at[t], load_sem.at[1 + t]
        )
        load.start()
        loads.append(load)

    load_list.wait()
    f = lists[lax.rem(box, 8), 0]
    column = lax.broadcasted_iota(jnp.int32, (points, face_size), 1)
    point = lax.broadcasted_iota(jnp.int32, (points, face_size), 0)
    target = 2 * stride * lax.rem(column, half) + stride * (column // half)
    pick[...] = jnp.where(point - target == f, 1.0, 0.0).astype(BF16)

    def strip(c):
        return pl.ds(pl.multiple_of(c * per, per), per)

    def cols(c):
        return pl.ds(pl.multiple_of(c * rows, rows), rows)

    for load in loads:
        load.wait()
    mine = []
    for par in range(2):
        picked = [kv[t, pl.ds(f + stride * par, per, stride=2 * stride), :] for t in range(tiles)]
        mine.append(jnp.concatenate(picked, axis=1))
        faces[0, par, strip(y), :] = mine[par]

    lane = lax.broadcasted_iota(jnp.int32, (per, points), 1)
    line = lax.broadcasted_iota(jnp.int32, (per, points), 0)
    place = lane - 2 * stride * (line + per * y) - f
    bands = []
    for off in range(3):
        total = jnp.zeros((1, points), F32)
        for par in range(2):
            hit = jnp.where(place == stride * (off + par), mine[par], 0.0)
            total += jnp.sum(hit, axis=0, keepdims=True)
        bands.append(total)
    spread = jnp.concatenate(bands + [jnp.zeros((5, points), F32)], axis=0)
    packed = jnp.zeros((8, face_size), F32)
    for _ in range(3):
        term = spread.astype(BF16)
        packed += dot(term, pick[...])
        spread = spread - term.astype(F32)
    band_send[...] = jnp.concatenate([packed[0:4, :half], packed[0:4, half:]], axis=0)
    pl.semaphore_wait(barrier, len(peers))

    started = []

    def send(src, dst, ssem, rsem, who):
        copy = pltpu.make_async_remote_copy(
            src_ref=src, dst_ref=dst, send_sem=ssem, recv_sem=rsem, device_id=who
        )
        copy.start()
        started.append(copy)

    def block(slot, fy, ry):
        return faces.at[slot, :, strip(fy), cols(ry)]

    def half_block(slot, par, fy, ry):
        return faces.at[slot, par, strip(fy), cols(ry)]

    def ring(way, k, ref):
        send(ref, ref, ring_ssem.at[way, k], ring_rsem.at[way, k], (down, up)[way])

    def staged(way, k, src, dst):
        send(src, dst, ring_ssem.at[way, k], ring_rsem.at[way, k], (down, up)[way])

    def ring_wait(way, k, ref):
        pltpu.make_async_remote_copy(
            src_ref=ref,
            dst_ref=ref,
            send_sem=ring_ssem.at[way, k],
            recv_sem=ring_rsem.at[way, k],
            device_id=(down, up)[way],
        ).wait_recv()

    def across(k, ref_of):
        send(ref_of(0), ref_of(1), die_ssem.at[k], die_rsem.at[k], sibling)

    def across_wait(k, ref_of):
        pltpu.make_async_remote_copy(
            src_ref=ref_of(0),
            dst_ref=ref_of(1),
            send_sem=die_ssem.at[k],
            recv_sem=die_rsem.at[k],
            device_id=sibling,
        ).wait_recv()

    for k, peer in peers[:-1]:
        send(band_send, band_recv.at[k], band_ssem.at[k], band_rsem.at[k], peer)

    ring(0, 0, block(0, y, y))
    ring(1, 0, block(0, y, y))

    at = lax.broadcasted_iota(jnp.int32, (per, rows), 1)
    kind = at - stride * ((at * 10923) >> 16)
    shared = kind == f
    side_cols = (ys[1], ys[3])

    def load_up(way, n, carrier):
        guest = faces[0, 1, strip(y), cols(side_cols[way])]
        stage[way, n] = jnp.where(shared, pltpu.roll(guest, rows - 1 - n, 1), carrier)

    for way in range(2):
        for par in range(2):
            load_up(way, par, faces[0, par, strip(y), cols(ys[2])])
        staged(way, 1, stage.at[way, pl.ds(0, 2)], block(0, y, ys[2]))
    for way in range(2):
        load_up(way, 4, faces[0, 0, strip(y), cols(side_cols[way])])
        staged(way, 4, stage.at[way, 4], half_block(0, 0, y, side_cols[way]))
    across(0, lambda s: faces.at[s, :, strip(y), :])

    def select(i, carry):
        part = pl.ds(pl.multiple_of(i * 128, 128), 128)
        high, low = split_two(jnp.concatenate([kv[t, part, :] for t in range(tiles)], axis=1))
        coupling[part, :] = dot(high, pick[...]) + dot(low, pick[...])
        return carry

    lax.fori_loop(0, rows // 128, select, 0)
    flipped = coupling[...].T
    for par in range(2):
        turned[par] = flipped[par * half:(par + 1) * half]
    for d in range(1, nblk):
        for par in range(2):
            faces[0, par, strip(ys[d]), cols(y)] = turned[par, strip(ys[d]), :]

    for way in range(2):
        for par in range(2):
            load_up(way, 2 + par, turned[par, strip(side_cols[way]), :])
        staged(way, 2, stage.at[way, pl.ds(2, 2)], block(0, side_cols[way], y))
    for d in range(1, nblk):
        across(d, lambda s, d=d: block(s, ys[d], y))

    def band_wait(k, peer):
        pltpu.make_async_remote_copy(
            src_ref=band_send,
            dst_ref=band_recv.at[k],
            send_sem=band_ssem.at[k],
            recv_sem=band_rsem.at[k],
            device_id=peer,
        ).wait_recv()

    own = band_send[...]
    for k, peer in peers[:-1]:
        band_wait(k, peer)
        own += band_recv[k]
    band_sum[...] = own
    send(band_sum, band_recv.at[0], band_ssem.at[0], band_rsem.at[0], sibling)
    band_wait(0, sibling)
    schur = own + band_recv[0]

    def wide(r):
        return jnp.broadcast_to(schur[r:r + 1], (8, half))

    a, b, c = wide(0), wide(5), wide(4)
    l00, l01, l10, l11 = wide(2), wide(1), jnp.zeros((8, half), F32), wide(6)
    steps = half.bit_length() - 1
    for step in range(steps):
        s = 1 << step

        def before(x, s=s):
            return pltpu.roll(x, s, 1)

        def after(x, s=s):
            return pltpu.roll(x, half - s, 1)

        scale = 1.0 / (a * c - b * b)
        ia, ib, ic = c * scale, -b * scale, a * scale
        iam, ibm, icm = before(ia), before(ib), before(ic)
        iap, ibp, icp = after(ia), after(ib), after(ic)
        m00, m01, m10, m11 = before(l00), before(l01), before(l10), before(l11)
        p00, p01, p10, p11 = after(l00), after(l01), after(l10), after(l11)
        g00, g01 = -(l00 * iam + l01 * ibm), -(l00 * ibm + l01 * icm)
        g10, g11 = -(l10 * iam + l11 * ibm), -(l10 * ibm + l11 * icm)
        h00, h01 = -(p00 * iap + p10 * ibp), -(p00 * ibp + p10 * icp)
        h10, h11 = -(p01 * iap + p11 * ibp), -(p01 * ibp + p11 * icp)
        for k, value in enumerate((g00, g01, g10, g11, h00, h01, h10, h11)):
            coef[step, k] = value
        a = a + g00 * l00 + g01 * l01 + h00 * p00 + h01 * p10
        b = b + g00 * l10 + g01 * l11 + h00 * p01 + h01 * p11
        c = c + g10 * l10 + g11 * l11 + h10 * p01 + h11 * p11
        l00, l01, l10, l11 = (
            g00 * m00 + g01 * m10,
            g00 * m01 + g01 * m11,
            g10 * m00 + g11 * m10,
            g10 * m01 + g11 * m11,
        )
    scale = 1.0 / (a * c - b * b)
    for k, value in enumerate((c * scale, -b * scale, a * scale)):
        last[k] = value

    def first(s):
        return block(s, ys[1], ys[1])

    def second(s):
        return block(s, ys[3], ys[3])

    ring_wait(0, 0, first(0))
    ring(0, 3, half_block(0, 0, ys[1], ys[1]))
    across(4, first)
    ring_wait(1, 0, second(0))
    ring(1, 3, half_block(0, 1, ys[3], ys[3]))
    across(5, second)

    tall = rows // 8

    def solve(i, carry):
        part = pl.ds(pl.multiple_of(i * 8 * tall, 8 * tall), 8 * tall)
        even = coupling[part, 0:half].reshape(tall, 8, half)
        odd = coupling[part, half:].reshape(tall, 8, half)
        for step in range(steps):
            s = 1 << step
            em, om = pltpu.roll(even, s, 2), pltpu.roll(odd, s, 2)
            ep, op = pltpu.roll(even, half - s, 2), pltpu.roll(odd, half - s, 2)
            g00, g01, g10, g11, h00, h01, h10, h11 = (coef[step, k] for k in range(8))
            even, odd = (
                even + g00 * em + g01 * om + h00 * ep + h01 * op,
                odd + g10 * em + g11 * om + h10 * ep + h11 * op,
            )
        wide_e = (last[0] * even + last[1] * odd).reshape(8 * tall, half)
        wide_o = (last[1] * even + last[2] * odd).reshape(8 * tall, half)
        for h, value in enumerate((wide_e, wide_o)):
            high, low = split_two(value)
            weights[0, part, h * half:(h + 1) * half] = high
            weights[1, part, h * half:(h + 1) * half] = low
        return carry

    lax.fori_loop(0, rows // (8 * tall), solve, 0)

    def merge(slot, ry):
        total = product(weights, faces[slot, :, :, cols(ry)].reshape(face_size, rows))
        side = core if slot == 0 else 1 - core
        place = pl.ds(pl.multiple_of(points * side + ry * rows, rows), rows)
        if slot == 0:
            wide_rows = rows // LANES
            own = [kv[ry * wide_rows + t] for t in range(wide_rows)]
            out[0, :, place] = jnp.concatenate(own, axis=1) - total
        else:
            out[0, :, place] = -total

    merge(0, y)
    across_wait(0, lambda s: faces.at[s, :, strip(y), :])
    for d in range(1, nblk):
        across_wait(d, lambda s, d=d: block(s, ys[d], y))
    merge(1, y)

    places = (
        ((ys[1], ys[3]), (ys[2], ys[1]), (ys[1], ys[2])),
        ((ys[3], ys[1]), (ys[2], ys[3]), (ys[3], ys[2])),
    )
    line = lax.broadcasted_iota(jnp.int32, (per, rows), 0)
    tile_lane = lax.broadcasted_iota(jnp.int32, (1, half), 1)

    def corner(par, fy, ry):
        above, below = ry == fy + 1, ry == fy - 1
        lane_of = jnp.where(above, ry, fy) * per
        p, q, r = (
            jnp.sum(jnp.where(tile_lane == lane_of, band_sum[k:k + 1, :], 0.0), axis=1, keepdims=True)
            for k in (2, 1, 6)
        )
        end = stride * (rows // stride - 1)
        if par == 0:
            spots = ((above, per - 1, 0, p), (below, 0, end - stride, p), (below, 0, end, q))
        else:
            spots = ((above, per - 1, 0, q), (above, per - 1, stride, r), (below, 0, end, r))
        value = jnp.zeros((per, rows), F32)
        for when, row, first_lane, entry in spots:
            hit = jnp.logical_and(line == row, at == jnp.where(when, first_lane + f, -1))
            value = jnp.where(hit, entry, value)
        return value

    def unload(way, n, par, fy, ry, guest, near):
        carrier = faces[0, par, strip(fy), cols(ry)]
        own_entries = corner(par, fy, ry) if near else 0.0
        faces[0, par, strip(fy), cols(ry)] = jnp.where(shared, own_entries, carrier)
        wanted = kind == jnp.where(f + 1 + n >= stride, f + 1 + n - stride, f + 1 + n)
        return jnp.where(wanted, pltpu.roll(carrier, 1 + n, 1), guest)

    far_of = lambda way: (lambda s: block(s, *places[way][0]))
    cross_of = lambda way: (lambda s: block(s, *places[way][1]))
    last_of = lambda way: (lambda s: block(s, *places[way][2]))
    half_of = lambda way: (lambda s: half_block(s, way, ys[2], ys[2]))

    for way in range(2):
        ring_wait(way, 1, far_of(way)(0))
        guest = corner(1, *places[way][2])
        for par in range(2):
            guest = unload(way, par, par, *places[way][0], guest, False)
        across(6 + way, far_of(way))
        faces[0, 1, strip(places[way][2][0]), cols(places[way][2][1])] = guest
    for way in range(2):
        fy, ry = places[way][2]
        ring_wait(way, 4, half_block(0, 0, fy, ry))
        guest = faces[0, 1, strip(fy), cols(ry)]
        guest = unload(way, 4, 0, fy, ry, guest, True)
        ring_wait(way, 2, cross_of(way)(0))
        for par in range(2):
            guest = unload(way, 2 + par, par, *places[way][1], guest, True)
        faces[0, 1, strip(fy), cols(ry)] = guest
        across(8 + way, cross_of(way))
        across(10 + way, last_of(way))
    merge(0, ys[1])
    merge(0, ys[3])
    across_wait(4, first)
    across_wait(5, second)
    for way in range(2):
        across_wait(6 + way, far_of(way))
        across_wait(8 + way, cross_of(way))
    merge(1, ys[1])
    merge(1, ys[3])
    for way in range(2):
        ring_wait(way, 3, half_of(way)(0))
        across(12 + way, half_of(way))
    merge(0, ys[2])
    for way in range(2):
        across_wait(10 + way, last_of(way))
        across_wait(12 + way, half_of(way))

    for copy in started:
        copy.wait_send()


def finish(nblk, partial, weights, faces, out, fresh, sems):
    _, rows, double = partial.shape
    points = double // 2
    face_size = weights.shape[2]
    core = lax.rem(lax.axis_index("box"), 2)
    y = lax.axis_index("blk")

    def place(side, c):
        return pl.ds(pl.multiple_of(points * side + c * rows, rows), rows)

    ready = []

    def write(k, src, where):
        copy = pltpu.make_async_copy(src, out.at[0, :, where], sems.at[k])
        copy.start()
        ready.append(copy)

    far = lax.rem(y + 2, nblk)
    for side in range(2):
        for n, d in enumerate((0, 1, 3)):
            where = place(side, lax.rem(y + d, nblk))
            write(3 * side + n, partial.at[0, :, where], where)
    where = place(core, far)
    write(6, partial.at[0, :, where], where)
    columns = pl.ds(pl.multiple_of(far * rows, rows), rows)
    fresh[...] = -product(weights, faces[1, :, :, columns].reshape(face_size, rows))
    write(7, fresh, place(1 - core, far))
    for copy in ready:
        copy.wait()


def solution(mesh):
    nblk = mesh.shape["blk"]

    def on_device(operator_map, face_list):
        _, rows, points = operator_map.shape
        face_size = face_list.shape[1]
        half = face_size // 2
        steps = half.bit_length() - 1
        dma = pltpu.SemaphoreType.DMA
        vmem = pl.BlockSpec(memory_space=pltpu.VMEM)
        shape = (1, rows, 2 * points)
        partial, weights, faces = pl.pallas_call(
            functools.partial(kernel, nblk),
            out_shape=(
                pltpu.VMEM(shape, F32),
                pltpu.VMEM((2, rows, face_size), BF16),
                pltpu.VMEM((2, 2, half, points), F32),
            ),
            in_specs=[pl.BlockSpec(memory_space=pltpu.HBM)] * 2,
            out_specs=(vmem, vmem, vmem),
            scratch_shapes=[
                pltpu.VMEM((points // LANES, rows, LANES), F32),
                pltpu.VMEM((points, face_size), BF16),
                pltpu.VMEM((rows, face_size), F32),
                pltpu.VMEM((2, half, rows), F32),
                pltpu.VMEM((2, 5, half // nblk, rows), F32),
                pltpu.VMEM((8, half), F32),
                pltpu.VMEM((8, half), F32),
                pltpu.VMEM((nblk, 8, half), F32),
                pltpu.VMEM((steps, 8, 8, half), F32),
                pltpu.VMEM((3, 8, half), F32),
                pltpu.SMEM((8, LANES), jnp.int32),
                dma((1 + points // LANES,)),
                dma((nblk,)),
                dma((nblk,)),
                dma((2, 5)),
                dma((2, 5)),
                dma((14,)),
                dma((14,)),
            ],
            compiler_params=pltpu.CompilerParams(
                collective_id=0, has_side_effects=True, vmem_limit_bytes=GRANT << 10
            ),
            name="gather_faces",
        )(operator_map, face_list)
        return pl.pallas_call(
            functools.partial(finish, nblk),
            out_shape=jax.ShapeDtypeStruct(shape, F32),
            in_specs=[vmem, vmem, vmem],
            out_specs=pl.BlockSpec(memory_space=pltpu.HBM),
            scratch_shapes=[pltpu.VMEM((rows, rows), F32), dma((8,))],
            compiler_params=pltpu.CompilerParams(vmem_limit_bytes=16 << 20),
            name="write_merged",
        )(partial, weights, faces)

    in_specs = (P("box", "blk", None), P())
    out_specs = P("box", "blk", None)
    return jax.shard_map(on_device, mesh=mesh, in_specs=in_specs, out_specs=out_specs, check_vma=False)
```

```python
import functools

import jax
import jax.numpy as jnp
from jax import lax
from jax.experimental import pallas as pl
from jax.experimental.pallas import tpu as pltpu
from jax.sharding import PartitionSpec as P

F32 = jnp.float32
BF16 = jnp.bfloat16
LANES = 128
GRANT = 51500


def split_two(x):
    high = x.astype(BF16)
    low = (x - high.astype(F32)).astype(BF16)
    return high, low


def dot(a, b):
    return jnp.dot(a, b, preferred_element_type=F32)


def product(weights, right):
    high, low = split_two(right)
    return dot(weights[0], high) + dot(weights[1], high) + dot(weights[0], low)


def kernel(
    nblk,
    map_hbm,
    list_hbm,
    out,
    weights,
    faces,
    kv0,
    kv1,
    kv2,
    kv3,
    pick,
    coupling,
    turned,
    stage,
    band_send,
    band_sum,
    band_recv,
    coef,
    last,
    lists,
    load_sem,
    band_ssem,
    band_rsem,
    ring_ssem,
    ring_rsem,
    die_ssem,
    die_rsem,
):
    kv = (kv0, kv1, kv2, kv3)
    wide_rows, rows, _ = kv0.shape
    points = nblk * rows
    face_size = pick.shape[1]
    half = face_size // 2
    per = half // nblk
    stride = points // face_size
    box = lax.axis_index("box")
    y = lax.axis_index("blk")
    core = lax.rem(box, 2)
    mate = box + 1 - 2 * core
    ys = [lax.rem(y + d, nblk) for d in range(nblk)]
    down, up, sibling = {"blk": ys[3]}, {"blk": ys[1]}, {"box": mate}

    peers = [(d, {"blk": ys[d]}) for d in range(1, nblk)] + [(0, {"box": mate})]
    barrier = pltpu.get_barrier_semaphore()
    for _, peer in peers:
        pl.semaphore_signal(barrier, inc=1, device_id=peer)
    group = pl.multiple_of((box // 8) * 8, 8)
    load_list = pltpu.make_async_copy(
        list_hbm.at[pl.ds(group, 8), pl.ds(0, 128)], lists, load_sem.at[0]
    )
    load_list.start()
    loads = []
    for d in range(nblk):
        for t in range(wide_rows):
            tile = ys[d] * wide_rows + t
            load = pltpu.make_async_copy(
                map_hbm.at[0, :, pl.ds(pl.multiple_of(tile * LANES, LANES), LANES)],
                kv[d].at[t],
                load_sem.at[1 + d * wide_rows + t],
            )
            load.start()
            loads.append(load)

    load_list.wait()
    f = lists[lax.rem(box, 8), 0]
    column = lax.broadcasted_iota(jnp.int32, (points, face_size), 1)
    point = lax.broadcasted_iota(jnp.int32, (points, face_size), 0)
    target = 2 * stride * lax.rem(column, half) + stride * (column // half)
    point = point + jnp.where(point >= points - y * rows, y * rows - points, y * rows)
    pick[...] = jnp.where(point - target == f, 1.0, 0.0).astype(BF16)

    def strip(c):
        return pl.ds(pl.multiple_of(c * per, per), per)

    def cols(c):
        return pl.ds(pl.multiple_of(c * rows, rows), rows)

    def pick_rows(d):
        found = []
        for load in loads[d * wide_rows:(d + 1) * wide_rows]:
            load.wait()
        for par in range(2):
            found.append(
                jnp.concatenate(
                    [
                        kv[d][t, pl.ds(f + stride * par, per, stride=2 * stride), :]
                        for t in range(wide_rows)
                    ],
                    axis=1,
                )
            )
            faces[0, par, strip(y), cols(ys[d])] = found[par]
        return found

    mine = pick_rows(0)
    follow = pick_rows(1)

    reach = [jnp.concatenate([mine[par], follow[par][:, :LANES]], axis=1) for par in range(2)]
    span = rows + LANES
    lane = lax.broadcasted_iota(jnp.int32, (per, span), 1)
    line = lax.broadcasted_iota(jnp.int32, (per, span), 0)
    place = lane - 2 * stride * line - f
    inside = jnp.where(y == nblk - 1, rows, span)
    bands = []
    for off in range(3):
        total = jnp.zeros((1, span), F32)
        for par in range(2):
            hit = jnp.logical_and(place == stride * (off + par), lane < inside)
            total += jnp.sum(jnp.where(hit, reach[par], 0.0), axis=0, keepdims=True)
        bands.append(total)
    spread = jnp.concatenate(bands + [jnp.zeros((5, span), F32)], axis=0)
    packed = jnp.zeros((8, face_size), F32)
    near, next_near = pick[0:rows, :], pick[rows:span, :]
    for _ in range(3):
        term = spread.astype(BF16)
        packed += dot(term[:, :rows], near) + dot(term[:, rows:], next_near)
        spread = spread - term.astype(F32)
    band_send[...] = jnp.concatenate([packed[0:4, :half], packed[0:4, half:]], axis=0)
    pl.semaphore_wait(barrier, len(peers))

    started = []

    def send(src, dst, ssem, rsem, who):
        copy = pltpu.make_async_remote_copy(
            src_ref=src, dst_ref=dst, send_sem=ssem, recv_sem=rsem, device_id=who
        )
        copy.start()
        started.append(copy)
        return copy

    def leave(copy):
        copy.wait_send()
        started[:] = [other for other in started if other is not copy]

    def block(slot, fy, ry):
        return faces.at[slot, :, strip(fy), cols(ry)]

    def half_block(slot, par, fy, ry):
        return faces.at[slot, par, strip(fy), cols(ry)]

    def ring(way, k, ref):
        return send(ref, ref, ring_ssem.at[way, k], ring_rsem.at[way, k], (down, up)[way])

    def staged(way, k, src, dst):
        return send(src, dst, ring_ssem.at[way, k], ring_rsem.at[way, k], (down, up)[way])

    def ring_wait(way, k, ref):
        pltpu.make_async_remote_copy(
            src_ref=ref,
            dst_ref=ref,
            send_sem=ring_ssem.at[way, k],
            recv_sem=ring_rsem.at[way, k],
            device_id=(down, up)[way],
        ).wait_recv()

    def across(k, ref_of):
        send(ref_of(0), ref_of(1), die_ssem.at[k], die_rsem.at[k], sibling)

    def across_wait(k, ref_of):
        pltpu.make_async_remote_copy(
            src_ref=ref_of(0),
            dst_ref=ref_of(1),
            send_sem=die_ssem.at[k],
            recv_sem=die_rsem.at[k],
            device_id=sibling,
        ).wait_recv()

    for k, peer in peers[:-1]:
        send(band_send, band_recv.at[k], band_ssem.at[k], band_rsem.at[k], peer)
    zeroth = [ring(way, 0, block(0, y, y)) for way in range(2)]
    for d in range(2, nblk):
        pick_rows(d)

    at = lax.broadcasted_iota(jnp.int32, (per, rows), 1)
    kind = at - stride * ((at * 10923) >> 16)
    shared = kind == f
    side_cols = (ys[1], ys[3])

    def load_up(way, n, carrier):
        guest = faces[0, 1, strip(y), cols(side_cols[way])]
        stage[way, n] = jnp.where(shared, pltpu.roll(guest, rows - 1 - n, 1), carrier)

    oneth = []
    for way in range(2):
        for par in range(2):
            load_up(way, par, faces[0, par, strip(y), cols(ys[2])])
        oneth.append(staged(way, 1, stage.at[way, pl.ds(0, 2)], block(0, y, ys[2])))
    for way in range(2):
        load_up(way, 4, faces[0, 0, strip(y), cols(side_cols[way])])
    across(0, lambda s: faces.at[s, :, strip(y), :])

    def select(i, carry):
        part = pl.ds(pl.multiple_of(i * 128, 128), 128)
        high, low = split_two(jnp.concatenate([kv[d][t, part, :] for d in range(nblk) for t in range(wide_rows)], axis=1))
        coupling[part, :] = dot(high, pick[...]) + dot(low, pick[...])
        return carry

    lax.fori_loop(0, rows // 128, select, 0)
    flipped = coupling[...].T
    for par in range(2):
        turned[par] = flipped[par * half:(par + 1) * half]
    for d in range(1, nblk):
        for par in range(2):
            faces[0, par, strip(ys[d]), cols(y)] = turned[par, strip(ys[d]), :]

    for way in range(2):
        for par in range(2):
            load_up(way, 2 + par, turned[par, strip(side_cols[way]), :])
    cross = []
    for way in range(2):
        leave(zeroth[way])
        cross.append(staged(way, 2, stage.at[way, pl.ds(2, 2)], block(0, side_cols[way], y)))
    for d in range(1, nblk):
        across(d, lambda s, d=d: block(s, ys[d], y))

    def band_wait(k, peer):
        pltpu.make_async_remote_copy(
            src_ref=band_send,
            dst_ref=band_recv.at[k],
            send_sem=band_ssem.at[k],
            recv_sem=band_rsem.at[k],
            device_id=peer,
        ).wait_recv()

    own = band_send[...]
    for k, peer in peers[:-1]:
        band_wait(k, peer)
        own += band_recv[k]
    band_sum[...] = own
    send(band_sum, band_recv.at[0], band_ssem.at[0], band_rsem.at[0], sibling)
    band_wait(0, sibling)
    schur = own + band_recv[0]

    def wide(r):
        return jnp.broadcast_to(schur[r:r + 1], (8, half))

    a, b, c = wide(0), wide(5), wide(4)
    l00, l01, l10, l11 = wide(2), wide(1), jnp.zeros((8, half), F32), wide(6)
    steps = half.bit_length() - 1
    for step in range(steps):
        s = 1 << step

        def before(x, s=s):
            return pltpu.roll(x, s, 1)

        def after(x, s=s):
            return pltpu.roll(x, half - s, 1)

        scale = 1.0 / (a * c - b * b)
        ia, ib, ic = c * scale, -b * scale, a * scale
        iam, ibm, icm = before(ia), before(ib), before(ic)
        iap, ibp, icp = after(ia), after(ib), after(ic)
        m00, m01, m10, m11 = before(l00), before(l01), before(l10), before(l11)
        p00, p01, p10, p11 = after(l00), after(l01), after(l10), after(l11)
        g00, g01 = -(l00 * iam + l01 * ibm), -(l00 * ibm + l01 * icm)
        g10, g11 = -(l10 * iam + l11 * ibm), -(l10 * ibm + l11 * icm)
        h00, h01 = -(p00 * iap + p10 * ibp), -(p00 * ibp + p10 * icp)
        h10, h11 = -(p01 * iap + p11 * ibp), -(p01 * ibp + p11 * icp)
        for k, value in enumerate((g00, g01, g10, g11, h00, h01, h10, h11)):
            coef[step, k] = value
        a = a + g00 * l00 + g01 * l01 + h00 * p00 + h01 * p10
        b = b + g00 * l10 + g01 * l11 + h00 * p01 + h01 * p11
        c = c + g10 * l10 + g11 * l11 + h10 * p01 + h11 * p11
        l00, l01, l10, l11 = (
            g00 * m00 + g01 * m10,
            g00 * m01 + g01 * m11,
            g10 * m00 + g11 * m10,
            g10 * m01 + g11 * m11,
        )
    scale = 1.0 / (a * c - b * b)
    for k, value in enumerate((c * scale, -b * scale, a * scale)):
        last[k] = value

    tall = rows // 8

    def solve(i, carry):
        part = pl.ds(pl.multiple_of(i * 8 * tall, 8 * tall), 8 * tall)
        even = coupling[part, 0:half].reshape(tall, 8, half)
        odd = coupling[part, half:].reshape(tall, 8, half)
        for step in range(steps):
            s = 1 << step
            em, om = pltpu.roll(even, s, 2), pltpu.roll(odd, s, 2)
            ep, op = pltpu.roll(even, half - s, 2), pltpu.roll(odd, half - s, 2)
            g00, g01, g10, g11, h00, h01, h10, h11 = (coef[step, k] for k in range(8))
            even, odd = (
                even + g00 * em + g01 * om + h00 * ep + h01 * op,
                odd + g10 * em + g11 * om + h10 * ep + h11 * op,
            )
        wide_e = (last[0] * even + last[1] * odd).reshape(8 * tall, half)
        wide_o = (last[1] * even + last[2] * odd).reshape(8 * tall, half)
        for h, value in enumerate((wide_e, wide_o)):
            high, low = split_two(value)
            weights[0, part, h * half:(h + 1) * half] = high
            weights[1, part, h * half:(h + 1) * half] = low
        return carry

    lax.fori_loop(0, rows // (8 * tall), solve, 0)

    def first(s):
        return block(s, ys[1], ys[1])

    def second(s):
        return block(s, ys[3], ys[3])

    for way in range(2):
        leave(oneth[way])
        staged(way, 4, stage.at[way, 4], half_block(0, 0, y, side_cols[way]))
    ring_wait(0, 0, first(0))
    across(4, first)
    ring_wait(1, 0, second(0))
    across(5, second)

    def merge(slot, d):
        ry = ys[d]
        total = product(weights, faces[slot, :, :, cols(ry)].reshape(face_size, rows))
        side = core if slot == 0 else 1 - core
        place = pl.ds(pl.multiple_of(points * side + ry * rows, rows), rows)
        if slot == 0:
            own = [kv[d][t] for t in range(wide_rows)]
            out[0, :, place] = jnp.concatenate(own, axis=1) - total
        else:
            out[0, :, place] = -total

    merge(0, 0)
    across_wait(0, lambda s: faces.at[s, :, strip(y), :])
    for d in range(1, nblk):
        across_wait(d, lambda s, d=d: block(s, ys[d], y))
    merge(1, 0)

    leave(cross[0])
    ring(0, 3, half_block(0, 0, ys[1], ys[1]))
    leave(cross[1])
    ring(1, 3, half_block(0, 1, ys[3], ys[3]))

    places = (
        ((ys[1], ys[3]), (ys[2], ys[1]), (ys[1], ys[2])),
        ((ys[3], ys[1]), (ys[2], ys[3]), (ys[3], ys[2])),
    )
    line = lax.broadcasted_iota(jnp.int32, (per, rows), 0)
    tile_lane = lax.broadcasted_iota(jnp.int32, (1, half), 1)

    def corner(par, fy, ry):
        above, below = ry == fy + 1, ry == fy - 1
        lane_of = jnp.where(above, ry, fy) * per
        p, q, r = (
            jnp.sum(jnp.where(tile_lane == lane_of, band_sum[k:k + 1, :], 0.0), axis=1, keepdims=True)
            for k in (2, 1, 6)
        )
        end = stride * (rows // stride - 1)
        if par == 0:
            spots = ((above, per - 1, 0, p), (below, 0, end - stride, p), (below, 0, end, q))
        else:
            spots = ((above, per - 1, 0, q), (above, per - 1, stride, r), (below, 0, end, r))
        value = jnp.zeros((per, rows), F32)
        for when, row, first_lane, entry in spots:
            hit = jnp.logical_and(line == row, at == jnp.where(when, first_lane + f, -1))
            value = jnp.where(hit, entry, value)
        return value

    def unload(way, n, par, fy, ry, guest, near):
        carrier = faces[0, par, strip(fy), cols(ry)]
        own_entries = corner(par, fy, ry) if near else 0.0
        faces[0, par, strip(fy), cols(ry)] = jnp.where(shared, own_entries, carrier)
        wanted = kind == jnp.where(f + 1 + n >= stride, f + 1 + n - stride, f + 1 + n)
        return jnp.where(wanted, pltpu.roll(carrier, 1 + n, 1), guest)

    far_of = lambda way: (lambda s: block(s, *places[way][0]))
    cross_of = lambda way: (lambda s: block(s, *places[way][1]))
    last_of = lambda way: (lambda s: block(s, *places[way][2]))
    half_of = lambda way: (lambda s: half_block(s, way, ys[2], ys[2]))

    for way in range(2):
        ring_wait(way, 1, far_of(way)(0))
        guest = corner(1, *places[way][2])
        for par in range(2):
            guest = unload(way, par, par, *places[way][0], guest, False)
        across(6 + way, far_of(way))
        faces[0, 1, strip(places[way][2][0]), cols(places[way][2][1])] = guest
    for way in range(2):
        fy, ry = places[way][2]
        ring_wait(way, 2, cross_of(way)(0))
        guest = faces[0, 1, strip(fy), cols(ry)]
        for par in range(2):
            guest = unload(way, 2 + par, par, *places[way][1], guest, True)
        across(8 + way, cross_of(way))
        faces[0, 1, strip(fy), cols(ry)] = guest
    merge(0, 1)
    merge(0, 3)
    for way in range(2):
        fy, ry = places[way][2]
        ring_wait(way, 4, half_block(0, 0, fy, ry))
        guest = faces[0, 1, strip(fy), cols(ry)]
        faces[0, 1, strip(fy), cols(ry)] = unload(way, 4, 0, fy, ry, guest, True)
        across(10 + way, last_of(way))
    for way in range(2):
        ring_wait(way, 3, half_of(way)(0))
        across(12 + way, half_of(way))
    across_wait(4, first)
    across_wait(5, second)
    for way in range(2):
        across_wait(6 + way, far_of(way))
        across_wait(8 + way, cross_of(way))
    merge(1, 1)
    merge(1, 3)
    merge(0, 2)
    for way in range(2):
        across_wait(10 + way, last_of(way))
        across_wait(12 + way, half_of(way))

    for copy in started:
        copy.wait_send()


def finish(nblk, partial, weights, faces, out, fresh, sems):
    _, rows, double = partial.shape
    points = double // 2
    face_size = weights.shape[2]
    core = lax.rem(lax.axis_index("box"), 2)
    y = lax.axis_index("blk")

    def place(side, c):
        return pl.ds(pl.multiple_of(points * side + c * rows, rows), rows)

    ready = []

    def write(k, src, where):
        copy = pltpu.make_async_copy(src, out.at[0, :, where], sems.at[k])
        copy.start()
        ready.append(copy)

    far = lax.rem(y + 2, nblk)
    for side in range(2):
        for n, d in enumerate((0, 1, 3)):
            where = place(side, lax.rem(y + d, nblk))
            write(3 * side + n, partial.at[0, :, where], where)
    where = place(core, far)
    write(6, partial.at[0, :, where], where)
    columns = pl.ds(pl.multiple_of(far * rows, rows), rows)
    fresh[...] = -product(weights, faces[1, :, :, columns].reshape(face_size, rows))
    write(7, fresh, place(1 - core, far))
    for copy in ready:
        copy.wait()


def solution(mesh):
    nblk = mesh.shape["blk"]

    def on_device(operator_map, face_list):
        _, rows, points = operator_map.shape
        face_size = face_list.shape[1]
        half = face_size // 2
        steps = half.bit_length() - 1
        dma = pltpu.SemaphoreType.DMA
        vmem = pl.BlockSpec(memory_space=pltpu.VMEM)
        shape = (1, rows, 2 * points)
        partial, weights, faces = pl.pallas_call(
            functools.partial(kernel, nblk),
            out_shape=(
                pltpu.VMEM(shape, F32),
                pltpu.VMEM((2, rows, face_size), BF16),
                pltpu.VMEM((2, 2, half, points), F32),
            ),
            in_specs=[pl.BlockSpec(memory_space=pltpu.HBM)] * 2,
            out_specs=(vmem, vmem, vmem),
            scratch_shapes=[
                *(pltpu.VMEM((rows // LANES, rows, LANES), F32) for _ in range(nblk)),
                pltpu.VMEM((points, face_size), BF16),
                pltpu.VMEM((rows, face_size), F32),
                pltpu.VMEM((2, half, rows), F32),
                pltpu.VMEM((2, 5, half // nblk, rows), F32),
                pltpu.VMEM((8, half), F32),
                pltpu.VMEM((8, half), F32),
                pltpu.VMEM((nblk, 8, half), F32),
                pltpu.VMEM((steps, 8, 8, half), F32),
                pltpu.VMEM((3, 8, half), F32),
                pltpu.SMEM((8, LANES), jnp.int32),
                dma((1 + points // LANES,)),
                dma((nblk,)),
                dma((nblk,)),
                dma((2, 5)),
                dma((2, 5)),
                dma((14,)),
                dma((14,)),
            ],
            compiler_params=pltpu.CompilerParams(
                collective_id=0, has_side_effects=True, vmem_limit_bytes=GRANT << 10
            ),
            name="gather_faces",
        )(operator_map, face_list)
        return pl.pallas_call(
            functools.partial(finish, nblk),
            out_shape=jax.ShapeDtypeStruct(shape, F32),
            in_specs=[vmem, vmem, vmem],
            out_specs=pl.BlockSpec(memory_space=pltpu.HBM),
            scratch_shapes=[pltpu.VMEM((rows, rows), F32), dma((8,))],
            compiler_params=pltpu.CompilerParams(vmem_limit_bytes=16 << 20),
            name="write_merged",
        )(partial, weights, faces)

    in_specs = (P("box", "blk", None), P())
    out_specs = P("box", "blk", None)
    return jax.shard_map(on_device, mesh=mesh, in_specs=in_specs, out_specs=out_specs, check_vma=False)
```

```python
import functools

import jax
import jax.numpy as jnp
from jax import lax
from jax.experimental import pallas as pl
from jax.experimental.pallas import tpu as pltpu
from jax.sharding import PartitionSpec as P

F32 = jnp.float32
BF16 = jnp.bfloat16
LANES = 128
GRANT = 51500


def split_two(x):
    high = x.astype(BF16)
    low = (x - high.astype(F32)).astype(BF16)
    return high, low


def dot(a, b):
    return jnp.dot(a, b, preferred_element_type=F32)


def product(weights, right):
    high, low = split_two(right)
    return dot(weights[0], high) + dot(weights[1], high) + dot(weights[0], low)


def kernel(
    nblk,
    map_hbm,
    list_hbm,
    out,
    weights,
    faces,
    kv0,
    kv1,
    kv2,
    kv3,
    pick,
    coupling,
    turned,
    stage,
    band_send,
    band_sum,
    band_recv,
    coef,
    last,
    lists,
    load_sem,
    band_ssem,
    band_rsem,
    ring_ssem,
    ring_rsem,
    die_ssem,
    die_rsem,
):
    kv = (kv0, kv1, kv2, kv3)
    wide_rows, rows, _ = kv0.shape
    points = nblk * rows
    face_size = pick.shape[1]
    half = face_size // 2
    per = half // nblk
    stride = points // face_size
    box = lax.axis_index("box")
    y = lax.axis_index("blk")
    core = lax.rem(box, 2)
    mate = box + 1 - 2 * core
    ys = [lax.rem(y + d, nblk) for d in range(nblk)]
    down, up, sibling = {"blk": ys[3]}, {"blk": ys[1]}, {"box": mate}

    peers = [(d, {"blk": ys[d]}) for d in range(1, nblk)] + [(0, {"box": mate})]
    others = [{"box": mate, "blk": ys[3]}, {"box": mate, "blk": ys[1]}]
    barrier = pltpu.get_barrier_semaphore()
    for _, peer in peers:
        pl.semaphore_signal(barrier, inc=1, device_id=peer)
    for peer in others:
        pl.semaphore_signal(barrier, inc=1, device_id=peer)
    group = pl.multiple_of((box // 8) * 8, 8)
    load_list = pltpu.make_async_copy(
        list_hbm.at[pl.ds(group, 8), pl.ds(0, 128)], lists, load_sem.at[0]
    )
    load_list.start()
    loads = []
    for d in range(nblk):
        for t in range(wide_rows):
            tile = ys[d] * wide_rows + t
            load = pltpu.make_async_copy(
                map_hbm.at[0, :, pl.ds(pl.multiple_of(tile * LANES, LANES), LANES)],
                kv[d].at[t],
                load_sem.at[1 + d * wide_rows + t],
            )
            load.start()
            loads.append(load)

    load_list.wait()
    f = lists[lax.rem(box, 8), 0]
    column = lax.broadcasted_iota(jnp.int32, (points, face_size), 1)
    point = lax.broadcasted_iota(jnp.int32, (points, face_size), 0)
    target = 2 * stride * lax.rem(column, half) + stride * (column // half)
    point = point + jnp.where(point >= points - y * rows, y * rows - points, y * rows)
    pick[...] = jnp.where(point - target == f, 1.0, 0.0).astype(BF16)

    def strip(c):
        return pl.ds(pl.multiple_of(c * per, per), per)

    def cols(c):
        return pl.ds(pl.multiple_of(c * rows, rows), rows)

    def pick_rows(d):
        found = []
        for load in loads[d * wide_rows:(d + 1) * wide_rows]:
            load.wait()
        for par in range(2):
            found.append(
                jnp.concatenate(
                    [
                        kv[d][t, pl.ds(f + stride * par, per, stride=2 * stride), :]
                        for t in range(wide_rows)
                    ],
                    axis=1,
                )
            )
            faces[0, par, strip(y), cols(ys[d])] = found[par]
        return found

    mine = pick_rows(0)
    follow = pick_rows(1)

    reach = [jnp.concatenate([mine[par], follow[par][:, :LANES]], axis=1) for par in range(2)]
    span = rows + LANES
    lane = lax.broadcasted_iota(jnp.int32, (per, span), 1)
    line = lax.broadcasted_iota(jnp.int32, (per, span), 0)
    place = lane - 2 * stride * line - f
    inside = jnp.where(y == nblk - 1, rows, span)
    bands = []
    for off in range(3):
        total = jnp.zeros((1, span), F32)
        for par in range(2):
            hit = jnp.logical_and(place == stride * (off + par), lane < inside)
            total += jnp.sum(jnp.where(hit, reach[par], 0.0), axis=0, keepdims=True)
        bands.append(total)
    spread = jnp.concatenate(bands + [jnp.zeros((5, span), F32)], axis=0)
    packed = jnp.zeros((8, face_size), F32)
    near, next_near = pick[0:rows, :], pick[rows:span, :]
    for _ in range(3):
        term = spread.astype(BF16)
        packed += dot(term[:, :rows], near) + dot(term[:, rows:], next_near)
        spread = spread - term.astype(F32)
    band_send[...] = jnp.concatenate([packed[0:4, :half], packed[0:4, half:]], axis=0)
    pl.semaphore_wait(barrier, len(peers) + len(others))

    started = []

    def send(src, dst, ssem, rsem, who):
        copy = pltpu.make_async_remote_copy(
            src_ref=src, dst_ref=dst, send_sem=ssem, recv_sem=rsem, device_id=who
        )
        copy.start()
        started.append(copy)
        return copy

    def leave(copy):
        copy.wait_send()
        started[:] = [other for other in started if other is not copy]

    def block(slot, fy, ry):
        return faces.at[slot, :, strip(fy), cols(ry)]

    def half_block(slot, par, fy, ry):
        return faces.at[slot, par, strip(fy), cols(ry)]

    def quarter(slot, par, fy, ry, n):
        size = per // 2
        return faces.at[slot, par, pl.ds(pl.multiple_of(fy * per + n * size, size), size), cols(ry)]

    def ring(way, k, ref):
        return send(ref, ref, ring_ssem.at[way, k], ring_rsem.at[way, k], (down, up)[way])

    def staged(way, k, src, dst):
        return send(src, dst, ring_ssem.at[way, k], ring_rsem.at[way, k], (down, up)[way])

    def ring_wait(way, k, ref):
        pltpu.make_async_remote_copy(
            src_ref=ref,
            dst_ref=ref,
            send_sem=ring_ssem.at[way, k],
            recv_sem=ring_rsem.at[way, k],
            device_id=(down, up)[way],
        ).wait_recv()

    def across(k, ref_of):
        send(ref_of(0), ref_of(1), die_ssem.at[k], die_rsem.at[k], sibling)

    def across_wait(k, ref_of):
        pltpu.make_async_remote_copy(
            src_ref=ref_of(0),
            dst_ref=ref_of(1),
            send_sem=die_ssem.at[k],
            recv_sem=die_rsem.at[k],
            device_id=sibling,
        ).wait_recv()

    for k, peer in peers[:-1]:
        send(band_send, band_recv.at[k], band_ssem.at[k], band_rsem.at[k], peer)
    zeroth = [ring(way, 0, block(0, y, y)) for way in range(2)]
    for d in range(2, nblk):
        pick_rows(d)

    at = lax.broadcasted_iota(jnp.int32, (per, rows), 1)
    kind = at - stride * ((at * 10923) >> 16)
    shared = kind == f
    side_cols = (ys[1], ys[3])

    def load_up(way, n, carrier):
        guest = faces[0, 1, strip(y), cols(side_cols[way])]
        stage[way, n] = jnp.where(shared, pltpu.roll(guest, rows - 1 - n, 1), carrier)

    oneth = []
    for way in range(2):
        for par in range(2):
            load_up(way, par, faces[0, par, strip(y), cols(ys[2])])
        oneth.append(staged(way, 1, stage.at[way, pl.ds(0, 2)], block(0, y, ys[2])))
    for way in range(2):
        load_up(way, 4, faces[0, 0, strip(y), cols(side_cols[way])])
    across(0, lambda s: faces.at[s, :, strip(y), :])

    def select(i, carry):
        part = pl.ds(pl.multiple_of(i * 128, 128), 128)
        high, low = split_two(jnp.concatenate([kv[d][t, part, :] for d in range(nblk) for t in range(wide_rows)], axis=1))
        coupling[part, :] = dot(high, pick[...]) + dot(low, pick[...])
        return carry

    lax.fori_loop(0, rows // 128, select, 0)
    flipped = coupling[...].T
    for par in range(2):
        turned[par] = flipped[par * half:(par + 1) * half]
    for d in range(1, nblk):
        for par in range(2):
            faces[0, par, strip(ys[d]), cols(y)] = turned[par, strip(ys[d]), :]

    for way in range(2):
        for par in range(2):
            load_up(way, 2 + par, turned[par, strip(side_cols[way]), :])
    cross = []
    for way in range(2):
        leave(zeroth[way])
        cross.append(staged(way, 2, stage.at[way, pl.ds(2, 2)], block(0, side_cols[way], y)))
    for d in range(1, nblk):
        across(d, lambda s, d=d: block(s, ys[d], y))

    def band_wait(k, peer):
        pltpu.make_async_remote_copy(
            src_ref=band_send,
            dst_ref=band_recv.at[k],
            send_sem=band_ssem.at[k],
            recv_sem=band_rsem.at[k],
            device_id=peer,
        ).wait_recv()

    own = band_send[...]
    for k, peer in peers[:-1]:
        band_wait(k, peer)
        own += band_recv[k]
    band_sum[...] = own
    send(band_sum, band_recv.at[0], band_ssem.at[0], band_rsem.at[0], sibling)
    band_wait(0, sibling)
    schur = own + band_recv[0]

    def wide(r):
        return jnp.broadcast_to(schur[r:r + 1], (8, half))

    a, b, c = wide(0), wide(5), wide(4)
    l00, l01, l10, l11 = wide(2), wide(1), jnp.zeros((8, half), F32), wide(6)
    steps = half.bit_length() - 1
    for step in range(steps):
        s = 1 << step

        def before(x, s=s):
            return pltpu.roll(x, s, 1)

        def after(x, s=s):
            return pltpu.roll(x, half - s, 1)

        scale = 1.0 / (a * c - b * b)
        ia, ib, ic = c * scale, -b * scale, a * scale
        iam, ibm, icm = before(ia), before(ib), before(ic)
        iap, ibp, icp = after(ia), after(ib), after(ic)
        m00, m01, m10, m11 = before(l00), before(l01), before(l10), before(l11)
        p00, p01, p10, p11 = after(l00), after(l01), after(l10), after(l11)
        g00, g01 = -(l00 * iam + l01 * ibm), -(l00 * ibm + l01 * icm)
        g10, g11 = -(l10 * iam + l11 * ibm), -(l10 * ibm + l11 * icm)
        h00, h01 = -(p00 * iap + p10 * ibp), -(p00 * ibp + p10 * icp)
        h10, h11 = -(p01 * iap + p11 * ibp), -(p01 * ibp + p11 * icp)
        for k, value in enumerate((g00, g01, g10, g11, h00, h01, h10, h11)):
            coef[step, k] = value
        a = a + g00 * l00 + g01 * l01 + h00 * p00 + h01 * p10
        b = b + g00 * l10 + g01 * l11 + h00 * p01 + h01 * p11
        c = c + g10 * l10 + g11 * l11 + h10 * p01 + h11 * p11
        l00, l01, l10, l11 = (
            g00 * m00 + g01 * m10,
            g00 * m01 + g01 * m11,
            g10 * m00 + g11 * m10,
            g10 * m01 + g11 * m11,
        )
    scale = 1.0 / (a * c - b * b)
    for k, value in enumerate((c * scale, -b * scale, a * scale)):
        last[k] = value

    tall = rows // 8

    def solve(i, carry):
        part = pl.ds(pl.multiple_of(i * 8 * tall, 8 * tall), 8 * tall)
        even = coupling[part, 0:half].reshape(tall, 8, half)
        odd = coupling[part, half:].reshape(tall, 8, half)
        for step in range(steps):
            s = 1 << step
            em, om = pltpu.roll(even, s, 2), pltpu.roll(odd, s, 2)
            ep, op = pltpu.roll(even, half - s, 2), pltpu.roll(odd, half - s, 2)
            g00, g01, g10, g11, h00, h01, h10, h11 = (coef[step, k] for k in range(8))
            even, odd = (
                even + g00 * em + g01 * om + h00 * ep + h01 * op,
                odd + g10 * em + g11 * om + h10 * ep + h11 * op,
            )
        wide_e = (last[0] * even + last[1] * odd).reshape(8 * tall, half)
        wide_o = (last[1] * even + last[2] * odd).reshape(8 * tall, half)
        for h, value in enumerate((wide_e, wide_o)):
            high, low = split_two(value)
            weights[0, part, h * half:(h + 1) * half] = high
            weights[1, part, h * half:(h + 1) * half] = low
        return carry

    lax.fori_loop(0, rows // (8 * tall), solve, 0)

    def first(s):
        return block(s, ys[1], ys[1])

    def second(s):
        return block(s, ys[3], ys[3])

    for way in range(2):
        leave(oneth[way])
        staged(way, 4, stage.at[way, 4], half_block(0, 0, y, side_cols[way]))
    ring_wait(0, 0, first(0))
    across(4, first)
    ring_wait(1, 0, second(0))
    across(5, second)

    def merge(slot, d):
        ry = ys[d]
        total = product(weights, faces[slot, :, :, cols(ry)].reshape(face_size, rows))
        side = core if slot == 0 else 1 - core
        place = pl.ds(pl.multiple_of(points * side + ry * rows, rows), rows)
        if slot == 0:
            own = [kv[d][t] for t in range(wide_rows)]
            out[0, :, place] = jnp.concatenate(own, axis=1) - total
        else:
            out[0, :, place] = -total

    merge(0, 0)
    across_wait(0, lambda s: faces.at[s, :, strip(y), :])
    for d in range(1, nblk):
        across_wait(d, lambda s, d=d: block(s, ys[d], y))
    merge(1, 0)

    passed = (ys[1], ys[3])
    ahead = []
    for way in range(2):
        leave(cross[way])
        ahead.append(ring(way, 3, quarter(0, way, passed[way], passed[way], 0)))

    places = (
        ((ys[1], ys[3]), (ys[2], ys[1]), (ys[1], ys[2])),
        ((ys[3], ys[1]), (ys[2], ys[3]), (ys[3], ys[2])),
    )
    line = lax.broadcasted_iota(jnp.int32, (per, rows), 0)
    tile_lane = lax.broadcasted_iota(jnp.int32, (1, half), 1)

    def corner(par, fy, ry):
        above, below = ry == fy + 1, ry == fy - 1
        lane_of = jnp.where(above, ry, fy) * per
        p, q, r = (
            jnp.sum(jnp.where(tile_lane == lane_of, band_sum[k:k + 1, :], 0.0), axis=1, keepdims=True)
            for k in (2, 1, 6)
        )
        end = stride * (rows // stride - 1)
        if par == 0:
            spots = ((above, per - 1, 0, p), (below, 0, end - stride, p), (below, 0, end, q))
        else:
            spots = ((above, per - 1, 0, q), (above, per - 1, stride, r), (below, 0, end, r))
        value = jnp.zeros((per, rows), F32)
        for when, row, first_lane, entry in spots:
            hit = jnp.logical_and(line == row, at == jnp.where(when, first_lane + f, -1))
            value = jnp.where(hit, entry, value)
        return value

    def unload(way, n, par, fy, ry, guest, near):
        carrier = faces[0, par, strip(fy), cols(ry)]
        own_entries = corner(par, fy, ry) if near else 0.0
        faces[0, par, strip(fy), cols(ry)] = jnp.where(shared, own_entries, carrier)
        wanted = kind == jnp.where(f + 1 + n >= stride, f + 1 + n - stride, f + 1 + n)
        return jnp.where(wanted, pltpu.roll(carrier, 1 + n, 1), guest)

    far_of = lambda way: (lambda s: block(s, *places[way][0]))
    cross_of = lambda way: (lambda s: block(s, *places[way][1]))
    last_of = lambda way: (lambda s: block(s, *places[way][2]))
    half_of = lambda way: (lambda s: quarter(s, way, ys[2], ys[2], 0))

    for way in range(2):
        ring_wait(way, 1, far_of(way)(0))
        guest = corner(1, *places[way][2])
        for par in range(2):
            guest = unload(way, par, par, *places[way][0], guest, False)
        across(6 + way, far_of(way))
        faces[0, 1, strip(places[way][2][0]), cols(places[way][2][1])] = guest
    for way in range(2):
        leave(ahead[way])
        beyond = quarter(0, way, passed[way], passed[way], 1)
        ring(way, 5, beyond)
        send(
            beyond,
            quarter(1, way, passed[way], passed[way], 1),
            ring_ssem.at[way, 6],
            ring_rsem.at[way, 6],
            others[way],
        )
    for way in range(2):
        fy, ry = places[way][2]
        ring_wait(way, 2, cross_of(way)(0))
        guest = faces[0, 1, strip(fy), cols(ry)]
        for par in range(2):
            guest = unload(way, 2 + par, par, *places[way][1], guest, True)
        across(8 + way, cross_of(way))
        faces[0, 1, strip(fy), cols(ry)] = guest
    merge(0, 1)
    merge(0, 3)
    for way in range(2):
        fy, ry = places[way][2]
        ring_wait(way, 4, half_block(0, 0, fy, ry))
        guest = faces[0, 1, strip(fy), cols(ry)]
        faces[0, 1, strip(fy), cols(ry)] = unload(way, 4, 0, fy, ry, guest, True)
        across(10 + way, last_of(way))
    for way in range(2):
        ring_wait(way, 3, half_of(way)(0))
        across(12 + way, half_of(way))
    across_wait(4, first)
    across_wait(5, second)
    for way in range(2):
        across_wait(6 + way, far_of(way))
        across_wait(8 + way, cross_of(way))
    merge(1, 1)
    merge(1, 3)
    for way in range(2):
        ring_wait(way, 5, quarter(0, way, ys[2], ys[2], 1))
    merge(0, 2)
    for way in range(2):
        pltpu.make_async_remote_copy(
            src_ref=quarter(0, way, ys[2], ys[2], 1),
            dst_ref=quarter(1, way, ys[2], ys[2], 1),
            send_sem=ring_ssem.at[way, 6],
            recv_sem=ring_rsem.at[way, 6],
            device_id=others[way],
        ).wait_recv()
    for way in range(2):
        across_wait(10 + way, last_of(way))
        across_wait(12 + way, half_of(way))

    for copy in started:
        copy.wait_send()


def finish(nblk, partial, weights, faces, out, fresh, sems):
    _, rows, double = partial.shape
    points = double // 2
    face_size = weights.shape[2]
    core = lax.rem(lax.axis_index("box"), 2)
    y = lax.axis_index("blk")

    def place(side, c):
        return pl.ds(pl.multiple_of(points * side + c * rows, rows), rows)

    ready = []

    def write(k, src, where):
        copy = pltpu.make_async_copy(src, out.at[0, :, where], sems.at[k])
        copy.start()
        ready.append(copy)

    far = lax.rem(y + 2, nblk)
    for side in range(2):
        for n, d in enumerate((0, 1, 3)):
            where = place(side, lax.rem(y + d, nblk))
            write(3 * side + n, partial.at[0, :, where], where)
    where = place(core, far)
    write(6, partial.at[0, :, where], where)
    columns = pl.ds(pl.multiple_of(far * rows, rows), rows)
    fresh[...] = -product(weights, faces[1, :, :, columns].reshape(face_size, rows))
    write(7, fresh, place(1 - core, far))
    for copy in ready:
        copy.wait()


def solution(mesh):
    nblk = mesh.shape["blk"]

    def on_device(operator_map, face_list):
        _, rows, points = operator_map.shape
        face_size = face_list.shape[1]
        half = face_size // 2
        steps = half.bit_length() - 1
        dma = pltpu.SemaphoreType.DMA
        vmem = pl.BlockSpec(memory_space=pltpu.VMEM)
        shape = (1, rows, 2 * points)
        partial, weights, faces = pl.pallas_call(
            functools.partial(kernel, nblk),
            out_shape=(
                pltpu.VMEM(shape, F32),
                pltpu.VMEM((2, rows, face_size), BF16),
                pltpu.VMEM((2, 2, half, points), F32),
            ),
            in_specs=[pl.BlockSpec(memory_space=pltpu.HBM)] * 2,
            out_specs=(vmem, vmem, vmem),
            scratch_shapes=[
                *(pltpu.VMEM((rows // LANES, rows, LANES), F32) for _ in range(nblk)),
                pltpu.VMEM((points, face_size), BF16),
                pltpu.VMEM((rows, face_size), F32),
                pltpu.VMEM((2, half, rows), F32),
                pltpu.VMEM((2, 5, half // nblk, rows), F32),
                pltpu.VMEM((8, half), F32),
                pltpu.VMEM((8, half), F32),
                pltpu.VMEM((nblk, 8, half), F32),
                pltpu.VMEM((steps, 8, 8, half), F32),
                pltpu.VMEM((3, 8, half), F32),
                pltpu.SMEM((8, LANES), jnp.int32),
                dma((1 + points // LANES,)),
                dma((nblk,)),
                dma((nblk,)),
                dma((2, 7)),
                dma((2, 7)),
                dma((14,)),
                dma((14,)),
            ],
            compiler_params=pltpu.CompilerParams(
                collective_id=0, has_side_effects=True, vmem_limit_bytes=GRANT << 10
            ),
            name="gather_faces",
        )(operator_map, face_list)
        return pl.pallas_call(
            functools.partial(finish, nblk),
            out_shape=jax.ShapeDtypeStruct(shape, F32),
            in_specs=[vmem, vmem, vmem],
            out_specs=pl.BlockSpec(memory_space=pltpu.HBM),
            scratch_shapes=[pltpu.VMEM((rows, rows), F32), dma((8,))],
            compiler_params=pltpu.CompilerParams(vmem_limit_bytes=16 << 20),
            name="write_merged",
        )(partial, weights, faces)

    in_specs = (P("box", "blk", None), P())
    out_specs = P("box", "blk", None)
    return jax.shard_map(on_device, mesh=mesh, in_specs=in_specs, out_specs=out_specs, check_vma=False)
```

```python
import functools

import jax
import jax.numpy as jnp
from jax import lax
from jax.experimental import pallas as pl
from jax.experimental.pallas import tpu as pltpu
from jax.sharding import PartitionSpec as P

F32 = jnp.float32
BF16 = jnp.bfloat16
LANES = 128
GRANT = 51500


def split_two(x):
    high = x.astype(BF16)
    low = (x - high.astype(F32)).astype(BF16)
    return high, low


def dot(a, b):
    return jnp.dot(a, b, preferred_element_type=F32)


def product(weights, right):
    high, low = split_two(right)
    return dot(weights[0], high) + dot(weights[1], high) + dot(weights[0], low)


def kernel(
    nblk,
    map_hbm,
    list_hbm,
    out,
    weights,
    faces,
    kv0,
    kv1,
    kv2,
    kv3,
    pick,
    coupling,
    turned,
    stage,
    band_send,
    band_sum,
    band_recv,
    coef,
    last,
    lists,
    load_sem,
    band_ssem,
    band_rsem,
    ring_ssem,
    ring_rsem,
    die_ssem,
    die_rsem,
):
    kv = (kv0, kv1, kv2, kv3)
    wide_rows, rows, _ = kv0.shape
    points = nblk * rows
    face_size = pick.shape[1]
    half = face_size // 2
    per = half // nblk
    stride = points // face_size
    box = lax.axis_index("box")
    y = lax.axis_index("blk")
    core = lax.rem(box, 2)
    mate = box + 1 - 2 * core
    ys = [lax.rem(y + d, nblk) for d in range(nblk)]
    down, up, sibling = {"blk": ys[3]}, {"blk": ys[1]}, {"box": mate}

    peers = [(d, {"blk": ys[d]}) for d in range(1, nblk)] + [(0, {"box": mate})]
    barrier = pltpu.get_barrier_semaphore()
    for _, peer in peers:
        pl.semaphore_signal(barrier, inc=1, device_id=peer)
    group = pl.multiple_of((box // 8) * 8, 8)
    load_list = pltpu.make_async_copy(
        list_hbm.at[pl.ds(group, 8), pl.ds(0, 128)], lists, load_sem.at[0]
    )
    load_list.start()
    loads = []
    for d in range(nblk):
        for t in range(wide_rows):
            tile = ys[d] * wide_rows + t
            load = pltpu.make_async_copy(
                map_hbm.at[0, :, pl.ds(pl.multiple_of(tile * LANES, LANES), LANES)],
                kv[d].at[t],
                load_sem.at[1 + d * wide_rows + t],
            )
            load.start()
            loads.append(load)

    load_list.wait()
    f = lists[lax.rem(box, 8), 0]
    column = lax.broadcasted_iota(jnp.int32, (points, face_size), 1)
    point = lax.broadcasted_iota(jnp.int32, (points, face_size), 0)
    target = 2 * stride * lax.rem(column, half) + stride * (column // half)
    point = point + jnp.where(point >= points - y * rows, y * rows - points, y * rows)
    pick[...] = jnp.where(point - target == f, 1.0, 0.0).astype(BF16)

    def strip(c):
        return pl.ds(pl.multiple_of(c * per, per), per)

    def cols(c):
        return pl.ds(pl.multiple_of(c * rows, rows), rows)

    def pick_rows(d):
        found = []
        for load in loads[d * wide_rows:(d + 1) * wide_rows]:
            load.wait()
        for par in range(2):
            found.append(
                jnp.concatenate(
                    [
                        kv[d][t, pl.ds(f + stride * par, per, stride=2 * stride), :]
                        for t in range(wide_rows)
                    ],
                    axis=1,
                )
            )
            faces[0, par, strip(y), cols(ys[d])] = found[par]
        return found

    mine = pick_rows(0)
    follow = pick_rows(1)

    reach = [jnp.concatenate([mine[par], follow[par][:, :LANES]], axis=1) for par in range(2)]
    span = rows + LANES
    lane = lax.broadcasted_iota(jnp.int32, (per, span), 1)
    line = lax.broadcasted_iota(jnp.int32, (per, span), 0)
    place = lane - 2 * stride * line - f
    inside = jnp.where(y == nblk - 1, rows, span)
    bands = []
    for off in range(3):
        total = jnp.zeros((1, span), F32)
        for par in range(2):
            hit = jnp.logical_and(place == stride * (off + par), lane < inside)
            total += jnp.sum(jnp.where(hit, reach[par], 0.0), axis=0, keepdims=True)
        bands.append(total)
    spread = jnp.concatenate(bands + [jnp.zeros((5, span), F32)], axis=0)
    packed = jnp.zeros((8, face_size), F32)
    near, next_near = pick[0:rows, :], pick[rows:span, :]
    for _ in range(3):
        term = spread.astype(BF16)
        packed += dot(term[:, :rows], near) + dot(term[:, rows:], next_near)
        spread = spread - term.astype(F32)
    band_send[...] = jnp.concatenate([packed[0:4, :half], packed[0:4, half:]], axis=0)
    pl.semaphore_wait(barrier, len(peers))

    started = []

    def send(src, dst, ssem, rsem, who):
        copy = pltpu.make_async_remote_copy(
            src_ref=src, dst_ref=dst, send_sem=ssem, recv_sem=rsem, device_id=who
        )
        copy.start()
        started.append(copy)
        return copy

    def leave(copy):
        copy.wait_send()
        started[:] = [other for other in started if other is not copy]

    def block(slot, fy, ry):
        return faces.at[slot, :, strip(fy), cols(ry)]

    def half_block(slot, par, fy, ry):
        return faces.at[slot, par, strip(fy), cols(ry)]

    def ring(way, k, ref):
        return send(ref, ref, ring_ssem.at[way, k], ring_rsem.at[way, k], (down, up)[way])

    def staged(way, k, src, dst):
        return send(src, dst, ring_ssem.at[way, k], ring_rsem.at[way, k], (down, up)[way])

    def ring_wait(way, k, ref):
        pltpu.make_async_remote_copy(
            src_ref=ref,
            dst_ref=ref,
            send_sem=ring_ssem.at[way, k],
            recv_sem=ring_rsem.at[way, k],
            device_id=(down, up)[way],
        ).wait_recv()

    def across(k, ref_of):
        send(ref_of(0), ref_of(1), die_ssem.at[k], die_rsem.at[k], sibling)

    def across_wait(k, ref_of):
        pltpu.make_async_remote_copy(
            src_ref=ref_of(0),
            dst_ref=ref_of(1),
            send_sem=die_ssem.at[k],
            recv_sem=die_rsem.at[k],
            device_id=sibling,
        ).wait_recv()

    for k, peer in peers[:-1]:
        send(band_send, band_recv.at[k], band_ssem.at[k], band_rsem.at[k], peer)
    zeroth = [ring(way, 0, block(0, y, y)) for way in range(2)]
    for d in range(2, nblk):
        pick_rows(d)

    at = lax.broadcasted_iota(jnp.int32, (per, rows), 1)
    kind = at - stride * ((at * 10923) >> 16)
    shared = kind == f
    side_cols = (ys[1], ys[3])

    def load_up(way, n, carrier):
        guest = faces[0, 1, strip(y), cols(side_cols[way])]
        stage[way, n] = jnp.where(shared, pltpu.roll(guest, rows - 1 - n, 1), carrier)

    oneth = []
    for way in range(2):
        for par in range(2):
            load_up(way, par, faces[0, par, strip(y), cols(ys[2])])
        oneth.append(staged(way, 1, stage.at[way, pl.ds(0, 2)], block(0, y, ys[2])))
    for way in range(2):
        load_up(way, 4, faces[0, 0, strip(y), cols(side_cols[way])])
    across(0, lambda s: faces.at[s, :, strip(y), :])

    def select(i, carry):
        part = pl.ds(pl.multiple_of(i * 128, 128), 128)
        high, low = split_two(jnp.concatenate([kv[d][t, part, :] for d in range(nblk) for t in range(wide_rows)], axis=1))
        coupling[part, :] = dot(high, pick[...]) + dot(low, pick[...])
        return carry

    lax.fori_loop(0, rows // 128, select, 0)
    flipped = coupling[...].T
    for par in range(2):
        turned[par] = flipped[par * half:(par + 1) * half]
    for d in range(1, nblk):
        for par in range(2):
            faces[0, par, strip(ys[d]), cols(y)] = turned[par, strip(ys[d]), :]

    for way in range(2):
        for par in range(2):
            load_up(way, 2 + par, turned[par, strip(side_cols[way]), :])
    cross = []
    for way in range(2):
        leave(zeroth[way])
        cross.append(staged(way, 2, stage.at[way, pl.ds(2, 2)], block(0, side_cols[way], y)))
    for d in range(1, nblk):
        across(d, lambda s, d=d: block(s, ys[d], y))

    def band_wait(k, peer):
        pltpu.make_async_remote_copy(
            src_ref=band_send,
            dst_ref=band_recv.at[k],
            send_sem=band_ssem.at[k],
            recv_sem=band_rsem.at[k],
            device_id=peer,
        ).wait_recv()

    own = band_send[...]
    for k, peer in peers[:-1]:
        band_wait(k, peer)
        own += band_recv[k]
    band_sum[...] = own
    send(band_sum, band_recv.at[0], band_ssem.at[0], band_rsem.at[0], sibling)
    band_wait(0, sibling)
    schur = own + band_recv[0]

    def wide(r):
        return jnp.broadcast_to(schur[r:r + 1], (8, half))

    a, b, c = wide(0), wide(5), wide(4)
    l00, l01, l10, l11 = wide(2), wide(1), jnp.zeros((8, half), F32), wide(6)
    steps = half.bit_length() - 1
    for step in range(steps):
        s = 1 << step

        def before(x, s=s):
            return pltpu.roll(x, s, 1)

        def after(x, s=s):
            return pltpu.roll(x, half - s, 1)

        scale = 1.0 / (a * c - b * b)
        ia, ib, ic = c * scale, -b * scale, a * scale
        iam, ibm, icm = before(ia), before(ib), before(ic)
        iap, ibp, icp = after(ia), after(ib), after(ic)
        m00, m01, m10, m11 = before(l00), before(l01), before(l10), before(l11)
        p00, p01, p10, p11 = after(l00), after(l01), after(l10), after(l11)
        g00, g01 = -(l00 * iam + l01 * ibm), -(l00 * ibm + l01 * icm)
        g10, g11 = -(l10 * iam + l11 * ibm), -(l10 * ibm + l11 * icm)
        h00, h01 = -(p00 * iap + p10 * ibp), -(p00 * ibp + p10 * icp)
        h10, h11 = -(p01 * iap + p11 * ibp), -(p01 * ibp + p11 * icp)
        for k, value in enumerate((g00, g01, g10, g11, h00, h01, h10, h11)):
            coef[step, k] = value
        a = a + g00 * l00 + g01 * l01 + h00 * p00 + h01 * p10
        b = b + g00 * l10 + g01 * l11 + h00 * p01 + h01 * p11
        c = c + g10 * l10 + g11 * l11 + h10 * p01 + h11 * p11
        l00, l01, l10, l11 = (
            g00 * m00 + g01 * m10,
            g00 * m01 + g01 * m11,
            g10 * m00 + g11 * m10,
            g10 * m01 + g11 * m11,
        )
    scale = 1.0 / (a * c - b * b)
    for k, value in enumerate((c * scale, -b * scale, a * scale)):
        last[k] = value

    tall = rows // 8

    def solve(i, carry):
        part = pl.ds(pl.multiple_of(i * 8 * tall, 8 * tall), 8 * tall)
        even = coupling[part, 0:half].reshape(tall, 8, half)
        odd = coupling[part, half:].reshape(tall, 8, half)
        for step in range(steps):
            s = 1 << step
            em, om = pltpu.roll(even, s, 2), pltpu.roll(odd, s, 2)
            ep, op = pltpu.roll(even, half - s, 2), pltpu.roll(odd, half - s, 2)
            g00, g01, g10, g11, h00, h01, h10, h11 = (coef[step, k] for k in range(8))
            even, odd = (
                even + g00 * em + g01 * om + h00 * ep + h01 * op,
                odd + g10 * em + g11 * om + h10 * ep + h11 * op,
            )
        wide_e = (last[0] * even + last[1] * odd).reshape(8 * tall, half)
        wide_o = (last[1] * even + last[2] * odd).reshape(8 * tall, half)
        for h, value in enumerate((wide_e, wide_o)):
            high, low = split_two(value)
            weights[0, part, h * half:(h + 1) * half] = high
            weights[1, part, h * half:(h + 1) * half] = low
        return carry

    lax.fori_loop(0, rows // (8 * tall), solve, 0)

    def first(s):
        return block(s, ys[1], ys[1])

    def second(s):
        return block(s, ys[3], ys[3])

    for way in range(2):
        leave(oneth[way])
        staged(way, 4, stage.at[way, 4], half_block(0, 0, y, side_cols[way]))
    ring_wait(0, 0, first(0))
    across(4, first)
    ring_wait(1, 0, second(0))
    across(5, second)

    def merge(slot, d):
        ry = ys[d]
        total = product(weights, faces[slot, :, :, cols(ry)].reshape(face_size, rows))
        side = core if slot == 0 else 1 - core
        place = pl.ds(pl.multiple_of(points * side + ry * rows, rows), rows)
        if slot == 0:
            own = [kv[d][t] for t in range(wide_rows)]
            out[0, :, place] = jnp.concatenate(own, axis=1) - total
        else:
            out[0, :, place] = -total

    merge(0, 0)
    across_wait(0, lambda s: faces.at[s, :, strip(y), :])
    for d in range(1, nblk):
        across_wait(d, lambda s, d=d: block(s, ys[d], y))
    leave(cross[0])
    ring(0, 3, half_block(0, 0, ys[1], ys[1]))
    leave(cross[1])
    ring(1, 3, half_block(0, 1, ys[3], ys[3]))
    merge(1, 0)


    places = (
        ((ys[1], ys[3]), (ys[2], ys[1]), (ys[1], ys[2])),
        ((ys[3], ys[1]), (ys[2], ys[3]), (ys[3], ys[2])),
    )
    line = lax.broadcasted_iota(jnp.int32, (per, rows), 0)
    tile_lane = lax.broadcasted_iota(jnp.int32, (1, half), 1)

    def corner(par, fy, ry):
        above, below = ry == fy + 1, ry == fy - 1
        lane_of = jnp.where(above, ry, fy) * per
        p, q, r = (
            jnp.sum(jnp.where(tile_lane == lane_of, band_sum[k:k + 1, :], 0.0), axis=1, keepdims=True)
            for k in (2, 1, 6)
        )
        end = stride * (rows // stride - 1)
        if par == 0:
            spots = ((above, per - 1, 0, p), (below, 0, end - stride, p), (below, 0, end, q))
        else:
            spots = ((above, per - 1, 0, q), (above, per - 1, stride, r), (below, 0, end, r))
        value = jnp.zeros((per, rows), F32)
        for when, row, first_lane, entry in spots:
            hit = jnp.logical_and(line == row, at == jnp.where(when, first_lane + f, -1))
            value = jnp.where(hit, entry, value)
        return value

    def unload(way, n, par, fy, ry, guest, near):
        carrier = faces[0, par, strip(fy), cols(ry)]
        own_entries = corner(par, fy, ry) if near else 0.0
        faces[0, par, strip(fy), cols(ry)] = jnp.where(shared, own_entries, carrier)
        wanted = kind == jnp.where(f + 1 + n >= stride, f + 1 + n - stride, f + 1 + n)
        return jnp.where(wanted, pltpu.roll(carrier, 1 + n, 1), guest)

    far_of = lambda way: (lambda s: block(s, *places[way][0]))
    cross_of = lambda way: (lambda s: block(s, *places[way][1]))
    last_of = lambda way: (lambda s: block(s, *places[way][2]))
    half_of = lambda way: (lambda s: half_block(s, way, ys[2], ys[2]))

    for way in range(2):
        ring_wait(way, 1, far_of(way)(0))
        guest = corner(1, *places[way][2])
        for par in range(2):
            guest = unload(way, par, par, *places[way][0], guest, False)
        across(6 + way, far_of(way))
        faces[0, 1, strip(places[way][2][0]), cols(places[way][2][1])] = guest
    for way in range(2):
        fy, ry = places[way][2]
        ring_wait(way, 2, cross_of(way)(0))
        guest = faces[0, 1, strip(fy), cols(ry)]
        for par in range(2):
            guest = unload(way, 2 + par, par, *places[way][1], guest, True)
        across(8 + way, cross_of(way))
        faces[0, 1, strip(fy), cols(ry)] = guest
    merge(0, 1)
    merge(0, 3)
    for way in range(2):
        fy, ry = places[way][2]
        ring_wait(way, 4, half_block(0, 0, fy, ry))
        guest = faces[0, 1, strip(fy), cols(ry)]
        faces[0, 1, strip(fy), cols(ry)] = unload(way, 4, 0, fy, ry, guest, True)
        across(10 + way, last_of(way))
    for way in range(2):
        ring_wait(way, 3, half_of(way)(0))
        across(12 + way, half_of(way))
    across_wait(4, first)
    across_wait(5, second)
    for way in range(2):
        across_wait(6 + way, far_of(way))
        across_wait(8 + way, cross_of(way))
    merge(1, 1)
    merge(1, 3)
    merge(0, 2)
    for way in range(2):
        across_wait(10 + way, last_of(way))
        across_wait(12 + way, half_of(way))

    for copy in started:
        copy.wait_send()


def finish(nblk, partial, weights, faces, out, fresh, sems):
    _, rows, double = partial.shape
    points = double // 2
    face_size = weights.shape[2]
    core = lax.rem(lax.axis_index("box"), 2)
    y = lax.axis_index("blk")

    def place(side, c):
        return pl.ds(pl.multiple_of(points * side + c * rows, rows), rows)

    ready = []

    def write(k, src, where):
        copy = pltpu.make_async_copy(src, out.at[0, :, where], sems.at[k])
        copy.start()
        ready.append(copy)

    far = lax.rem(y + 2, nblk)
    for side in range(2):
        for n, d in enumerate((0, 1, 3)):
            where = place(side, lax.rem(y + d, nblk))
            write(3 * side + n, partial.at[0, :, where], where)
    where = place(core, far)
    write(6, partial.at[0, :, where], where)
    columns = pl.ds(pl.multiple_of(far * rows, rows), rows)
    fresh[...] = -product(weights, faces[1, :, :, columns].reshape(face_size, rows))
    write(7, fresh, place(1 - core, far))
    for copy in ready:
        copy.wait()


def solution(mesh):
    nblk = mesh.shape["blk"]

    def on_device(operator_map, face_list):
        _, rows, points = operator_map.shape
        face_size = face_list.shape[1]
        half = face_size // 2
        steps = half.bit_length() - 1
        dma = pltpu.SemaphoreType.DMA
        vmem = pl.BlockSpec(memory_space=pltpu.VMEM)
        shape = (1, rows, 2 * points)
        partial, weights, faces = pl.pallas_call(
            functools.partial(kernel, nblk),
            out_shape=(
                pltpu.VMEM(shape, F32),
                pltpu.VMEM((2, rows, face_size), BF16),
                pltpu.VMEM((2, 2, half, points), F32),
            ),
            in_specs=[pl.BlockSpec(memory_space=pltpu.HBM)] * 2,
            out_specs=(vmem, vmem, vmem),
            scratch_shapes=[
                *(pltpu.VMEM((rows // LANES, rows, LANES), F32) for _ in range(nblk)),
                pltpu.VMEM((points, face_size), BF16),
                pltpu.VMEM((rows, face_size), F32),
                pltpu.VMEM((2, half, rows), F32),
                pltpu.VMEM((2, 5, half // nblk, rows), F32),
                pltpu.VMEM((8, half), F32),
                pltpu.VMEM((8, half), F32),
                pltpu.VMEM((nblk, 8, half), F32),
                pltpu.VMEM((steps, 8, 8, half), F32),
                pltpu.VMEM((3, 8, half), F32),
                pltpu.SMEM((8, LANES), jnp.int32),
                dma((1 + points // LANES,)),
                dma((nblk,)),
                dma((nblk,)),
                dma((2, 5)),
                dma((2, 5)),
                dma((14,)),
                dma((14,)),
            ],
            compiler_params=pltpu.CompilerParams(
                collective_id=0, has_side_effects=True, vmem_limit_bytes=GRANT << 10
            ),
            name="gather_faces",
        )(operator_map, face_list)
        return pl.pallas_call(
            functools.partial(finish, nblk),
            out_shape=jax.ShapeDtypeStruct(shape, F32),
            in_specs=[vmem, vmem, vmem],
            out_specs=pl.BlockSpec(memory_space=pltpu.HBM),
            scratch_shapes=[pltpu.VMEM((rows, rows), F32), dma((8,))],
            compiler_params=pltpu.CompilerParams(vmem_limit_bytes=16 << 20),
            name="write_merged",
        )(partial, weights, faces)

    in_specs = (P("box", "blk", None), P())
    out_specs = P("box", "blk", None)
    return jax.shard_map(on_device, mesh=mesh, in_specs=in_specs, out_specs=out_specs, check_vma=False)
```
